32 devices in a mesh: wide: 8 (over z, y), narrow: 4 (over x, core).
Axes of the slice: x: 2, y: 2, z: 4, core: 2. Of those that a mesh axis runs over, the one named last changes fastest.
Arguments:
- face_blocks: float32 [1280, 320, 320], P(('wide', 'narrow')), may hold values from -0.3125 to 0.3125
- face_elems: int32 [1280, 2], P(('wide', 'narrow')), may hold values from 0 to 255, as said below
- coarse_slot: int32 [256], replicated, may hold values from 0 to 255, as said below
- prolong: float32 [320, 135], replicated, may hold values from -0.3125 to 0.3125
- fine_residual: float32 [256, 320], P(('wide', 'narrow')), may hold values from -6 to 6
- block_inverse: float32 [256, 135, 135], P(('wide', 'narrow'))
Outputs:
- fine_correction: float32 [256, 320], P(('wide', 'narrow'))
- owned_blocks: float32 [2560, 135, 135], P(('wide', 'narrow'))
The draws below stay inside these ranges and needn't reach their ends.
Inputs may be any that keep to these rules, and one draw needn't show every extreme that they name: `coarse_slot`: A permutation: every element has its own coarse row. `face_elems`: the row and column elements of a face differ. With the owner of an element being coarse_slot // 32, among the 40 faces of each device (aligned blocks of 40 rows, devices in the order wide then narrow) at most 10 have row elements of any one owner, and for each narrow index one owner takes exactly 10 faces from every device with that narrow index.
All inputs are finite; a program needn't handle non-finite values.
Results may differ from the reference program's by a relative error of at most 0.000075.
Values sent between devices are 32-bit elements; how exact they have to be, the bound alone decides.
No kernel may reach another device: no remote copies, remote signals or barrier semaphores. Data moves between devices by JAX's collectives and lax.ppermute only.
A program may use at most 192 MiB of HBM per device.

```python
import jax
import jax.numpy as jnp
from jax import lax

NF = 320
NC = 135
FACE_DEV = 40
EL_DEV = 8
CAP = 10
FACES = 1280
ELEMS = 256
EL_OWN = 32
N_WIDE = 8
N_NARROW = 4


def face_pattern(key):
    keys = jax.random.split(jax.random.fold_in(key, 7), 6)
    slot_table = jax.random.permutation(keys[0], ELEMS).astype(jnp.int32)
    inverse = jnp.argsort(slot_table).astype(jnp.int32)
    block_count = N_WIDE * N_NARROW
    narrow_of = jnp.arange(block_count, dtype=jnp.int32) % N_NARROW
    hottest = jax.random.randint(keys[1], (N_NARROW,), 0, N_WIDE, dtype=jnp.int32)[narrow_of]
    spread_len = (N_WIDE - 1) * CAP
    spread_idx = jnp.arange(spread_len, dtype=jnp.int32)
    candidate = (hottest[:, None] + 1 + spread_idx[None, :] // CAP) % N_WIDE
    scores = jax.random.randint(keys[2], (block_count, spread_len), 0, 65536, dtype=jnp.int32) * spread_len + spread_idx[None, :]
    shuffled = jnp.take_along_axis(candidate, jnp.argsort(scores, axis=1), axis=1)[:, :FACE_DEV - CAP]
    owners = jnp.concatenate([jnp.broadcast_to(hottest[:, None], (block_count, CAP)), shuffled], axis=1)
    face_idx = jnp.arange(FACE_DEV, dtype=jnp.int32)
    scores_two = jax.random.randint(keys[3], (block_count, FACE_DEV), 0, 65536, dtype=jnp.int32) * FACE_DEV + face_idx[None, :]
    owners = jnp.take_along_axis(owners, jnp.argsort(scores_two, axis=1), axis=1).reshape(-1)
    row_slot = owners * EL_OWN + jax.random.randint(keys[4], (FACES,), 0, EL_OWN, dtype=jnp.int32)
    col_slot = (row_slot + jax.random.randint(keys[5], (FACES,), 1, ELEMS, dtype=jnp.int32)) % ELEMS
    pairs = jnp.stack([inverse[row_slot], inverse[col_slot]], axis=1).astype(jnp.int32)
    return (slot_table, pairs)


def draw_face_elems(key, part):
    return face_pattern(key)[1]


def draw_coarse_slot(key, part):
    return face_pattern(key)[0]


def draw_block_inverse(key, part):
    keys = jax.random.split(jax.random.fold_in(key, 11), 2)
    identity = (jnp.arange(NC)[:, None] == jnp.arange(NC)[None, :]).astype(jnp.float32)
    noise = jax.random.normal(keys[0], (ELEMS, NC, NC), jnp.float32) * (0.5 * NC ** (-0.5))
    diagonal = 1.0 + jax.random.uniform(keys[1], (ELEMS, 1, 1), jnp.float32, -0.2, 0.2)
    return (diagonal * identity + noise).astype(jnp.float32)


def level_of(rng, extent, shards, low, largest):
    gain, own = 1.0, jax.random.fold_in(rng, 6)
    for axis_at, shards_of in shards:
        draws = jnp.exp(jax.random.uniform(jax.random.fold_in(own, axis_at), (shards_of,), jnp.float32, low / len(shards), largest / len(shards)))
        gain = gain * jnp.repeat(draws, extent[axis_at] // shards_of).reshape([-1 if axis == axis_at else 1 for axis in range(len(extent))])
    return gain


def scatter_about(stream_key, dims, scale, most, cuts=(), kind=jnp.bfloat16):
    loudness = level_of(stream_key, dims, cuts, -0.22, 0.18) if cuts else 1.0
    drawn = jax.random.normal(stream_key, dims, jnp.float32) * scale * loudness
    return jnp.minimum(jnp.maximum(drawn, -most), most).astype(kind)


def setup_inputs(seed: int = 0) -> dict:
    arg_keys = jax.random.split(jax.random.key(seed), 7)
    face_blocks = scatter_about(arg_keys[0], (FACES, NF, NF), (0.6 * (NC * FACE_DEV // EL_DEV) ** -0.5), 0.3125, ((0, 32),), jnp.float32)
    face_elems = draw_face_elems(jax.random.fold_in(arg_keys[6], 71), 0)
    coarse_slot = draw_coarse_slot(jax.random.fold_in(arg_keys[6], 71), 0)
    prolong = scatter_about(arg_keys[3], (NF, NC), NF ** -0.5, 0.3125, (), jnp.float32)
    fine_residual = scatter_about(arg_keys[4], (ELEMS, NF), 1.0, 6.0, ((0, 32),), jnp.float32)
    block_inverse = draw_block_inverse(jax.random.fold_in(arg_keys[6], 71), 0)
    return dict(face_blocks=face_blocks, face_elems=face_elems, coarse_slot=coarse_slot, prolong=prolong, fine_residual=fine_residual, block_inverse=block_inverse)


DAMPING = 0.7
PRECISE = lax.Precision.HIGHEST


def face_terms(inputs, prolong):
    blocks, vectors = inputs
    applied = jnp.einsum("fij,jc->fic", blocks, prolong, precision=PRECISE)
    coarse_blocks = jnp.einsum("ia,fic->fac", prolong, applied, precision=PRECISE)
    products = jnp.einsum("fac,fc->fa", coarse_blocks, vectors, precision=PRECISE)
    return coarse_blocks, products


def partial_terms(prolong):
    def apply_group(inputs):
        return face_terms(inputs, prolong)
    return apply_group


def reference(face_blocks, face_elems, coarse_slot, prolong, fine_residual, block_inverse):
    device_count = N_WIDE * N_NARROW
    coarse_rhs = jnp.dot(fine_residual, prolong, precision=PRECISE)
    sweep_one = DAMPING * jnp.einsum("snm,sm->sn", block_inverse, coarse_rhs, precision=PRECISE)
    slot_pairs = jnp.take(coarse_slot, face_elems, axis=0)
    row_slot = slot_pairs[:, 0]
    col_slot = slot_pairs[:, 1]
    column_values = jnp.take(sweep_one, col_slot, axis=0)
    grouped_blocks = face_blocks.reshape(device_count, FACE_DEV, NF, NF)
    grouped_values = column_values.reshape(device_count, FACE_DEV, NC)
    blocks_all, contributions = lax.map(partial_terms(prolong), (grouped_blocks, grouped_values))
    coupling = jax.ops.segment_sum(contributions.reshape(-1, NC), row_slot, num_segments=ELEMS)
    update = (1.0 - DAMPING) * coarse_rhs - coupling
    sweep_two = sweep_one + DAMPING * jnp.einsum("snm,sm->sn", block_inverse, update, precision=PRECISE)
    correction = jnp.dot(sweep_two, prolong.T, precision=PRECISE)

    owner_of = (row_slot // EL_OWN).astype(jnp.int32).reshape(device_count, FACE_DEV)
    selector = (owner_of[:, :, None] == jnp.arange(N_WIDE, dtype=jnp.int32)[None, None, :]).astype(jnp.int32)
    ranking = jnp.sum(selector * (jnp.cumsum(selector, axis=1) - 1), axis=2)
    device = jnp.arange(device_count, dtype=jnp.int32)[:, None]
    wide_of = device // N_NARROW
    narrow_of = device % N_NARROW
    placing = (((owner_of * N_NARROW + narrow_of) * N_WIDE + wide_of) * CAP + ranking).astype(jnp.int32)
    owned = jnp.zeros((device_count * N_WIDE * CAP, NC, NC), jnp.float32)
    owned = owned.at[placing.reshape(-1)].set(blocks_all.reshape(-1, NC, NC))
    return correction, owned
```

```python
import functools

import jax
import jax.numpy as jnp
from jax import lax
from jax.experimental import pallas as pl
from jax.experimental.pallas import tpu as pltpu
from jax.sharding import PartitionSpec as P

DAMPING = 0.7
PRECISE = lax.Precision.HIGHEST
BOTH = ("wide", "narrow")
LANES = 128
F32 = jnp.float32
BF16 = jnp.bfloat16


def round_up(value, unit):
    return (value + unit - 1) // unit * unit


def place_kernel(owner_rows, cap, wide, chunks, elems, slots, fetch, valid, row, col, count, table):
    faces = elems.shape[1]
    total = wide * cap

    def clear(i, c):
        count[i] = 0
        return c

    def empty(i, c):
        table[i] = -1
        return c

    def put(f, c):
        r = slots[elems[0, f]]
        row[f] = r
        col[f] = slots[elems[1, f]]
        owner = lax.div(r, owner_rows)
        rank = count[owner]
        count[owner] = rank + 1
        table[owner * cap + rank] = f
        return c

    lax.fori_loop(0, wide, clear, 0)
    lax.fori_loop(0, total, empty, 0)
    lax.fori_loop(0, faces, put, 0)
    at, first = 0, 0
    for ranks in chunks:

        def take(i, last, at=at, first=first, ranks=ranks):
            f = table[lax.div(i, ranks) * cap + first + lax.rem(i, ranks)]
            here = f >= 0
            last = jnp.where(here, f, last)
            valid[at + i] = here.astype(jnp.int32)
            fetch[at + i] = last
            return last

        lax.fori_loop(0, wide * ranks, take, jnp.int32(0))
        at += wide * ranks
        first += ranks


def place_faces(face_elems, coarse_slot, owner_rows, cap, wide, chunks):
    faces = face_elems.shape[0]
    total = wide * cap
    smem = pl.BlockSpec(memory_space=pltpu.SMEM)
    shape = lambda n: jax.ShapeDtypeStruct((n,), jnp.int32)
    return pl.pallas_call(
        functools.partial(place_kernel, owner_rows, cap, wide, chunks),
        out_shape=(shape(total), shape(total), shape(faces), shape(faces)),
        in_specs=[smem, smem],
        out_specs=(smem, smem, smem, smem),
        scratch_shapes=[pltpu.SMEM((wide,), jnp.int32), pltpu.SMEM((total,), jnp.int32)],
        name="place_faces",
    )(face_elems.T, coarse_slot)


def split(x):
    high = x.astype(BF16)
    return high, (x - high.astype(F32)).astype(BF16)


def dot3(a, b):
    (ah, al), (bh, bl) = a, b
    dot = functools.partial(jnp.dot, preferred_element_type=F32)
    return dot(ah, bh) + (dot(al, bh) + dot(ah, bl))


def galerkin_kernel(rows_main, fetch, valid, a_ref, p_ref, pt_ref, o_ref, ph, pl_, th, tl):
    step = pl.program_id(0)

    @pl.when(step == 0)
    def _():
        ph[...], pl_[...] = split(p_ref[...])
        th[...], tl[...] = split(pt_ref[...])

    @pl.when(valid[step] == 0)
    def _():
        o_ref[...] = jnp.zeros_like(o_ref)

    @pl.when(valid[step] != 0)
    def _():
        applied = dot3(split(a_ref[0]), (ph[...], pl_[...]))
        block = dot3((th[...], tl[...]), split(applied))
        o_ref[0, :rows_main, :] = block[:, :LANES]
        right = block[:, LANES:]
        turned = right[:LANES].T[:8]
        corner = pltpu.roll(right[LANES:rows_main], 0, 1, stride=8, stride_axis=0)
        corner = jnp.sum(corner, axis=0, keepdims=True)
        last = lax.broadcasted_iota(jnp.int32, (8, LANES), 0) == 7
        o_ref[0, rows_main:, :] = jnp.where(last, corner, turned)


def galerkin(face_blocks, p_pad, pt_pad, fetch, valid, wide, ranks):
    fine = face_blocks.shape[1]
    rows_main, width = pt_pad.shape[0], p_pad.shape[1]
    rows = rows_main + 8
    steps = wide * ranks
    out = pl.pallas_call(
        functools.partial(galerkin_kernel, rows_main),
        out_shape=jax.ShapeDtypeStruct((steps, rows, LANES), F32),
        grid_spec=pltpu.PrefetchScalarGridSpec(
            num_scalar_prefetch=2,
            grid=(steps,),
            in_specs=[
                pl.BlockSpec((1, fine, fine), lambda s, fetch, valid: (fetch[s], 0, 0)),
                pl.BlockSpec((fine, width), lambda s, fetch, valid: (0, 0)),
                pl.BlockSpec((rows_main, fine), lambda s, fetch, valid: (0, 0)),
            ],
            out_specs=pl.BlockSpec((1, rows, LANES), lambda s, fetch, valid: (s, 0, 0)),
            scratch_shapes=[
                pltpu.VMEM((fine, width), BF16),
                pltpu.VMEM((fine, width), BF16),
                pltpu.VMEM((rows_main, fine), BF16),
                pltpu.VMEM((rows_main, fine), BF16),
            ],
        ),
        cost_estimate=pl.CostEstimate(
            flops=steps * 4 * 6 * fine * fine * width // 10,
            bytes_accessed=steps * 4 * (fine * fine // 2 + rows * LANES),
            transcendentals=0,
        ),
        name="galerkin",
    )(fetch, valid, face_blocks, p_pad, pt_pad)
    return out.reshape(wide, ranks, rows, LANES)


def unpack_kernel(chunks, cap, coarse, *refs):
    count = len(chunks)
    parts, out = refs[:count], refs[count]
    tiles, turned, tile_sem, turned_sem = refs[count + 1 :]
    step, steps = pl.program_id(0), pl.num_programs(0)
    wide = parts[0].shape[0]
    total = wide * cap

    def copies(source_row, target, sem):
        first = 0
        for part, ranks in zip(parts, chunks):
            yield pltpu.make_async_copy(
                part.at[:, :, pl.ds(source_row, 8), :],
                target.at[:, pl.ds(first, ranks)],
                sem,
            )
            first += ranks

    def fetch(tile, buffer):
        return copies(pl.multiple_of(tile * 8, 8), tiles.at[buffer], tile_sem.at[buffer])

    def rows_of(block, k):
        rows = block.reshape(total * 8, LANES)[pl.ds(k, total, stride=8), :]
        if total < LANES:
            rows = jnp.concatenate([rows, jnp.zeros((LANES - total, LANES), F32)], axis=0)
        return rows.T

    buffer = lax.rem(step, 2)

    @pl.when(step == 0)
    def _():
        last = tiles.at[1]
        for copy in copies(steps * 8, last, tile_sem.at[1]):
            copy.start()
        for copy in fetch(0, 0):
            copy.start()
        for copy in copies(steps * 8, last, tile_sem.at[1]):
            copy.wait()
        for k in range(8):
            turns = rows_of(last, k)
            if k < 7:
                turned[pl.ds(k, LANES, stride=8), :] = turns
            else:
                turned[pl.ds(8 * LANES, 64), :] = turns[:64]

    @pl.when(step + 1 < steps)
    def _():
        for copy in fetch(step + 1, 1 - buffer):
            copy.start()

    for copy in fetch(step, buffer):
        copy.wait()
    block = tiles.at[buffer]
    for k in range(8):
        out[k, :LANES, :] = rows_of(block, k)[:, :total]
        out[k, LANES:coarse, :] = turned[pl.ds(pl.multiple_of((step * 8 + k) * 8, 8), 8), :][
            : coarse - LANES, :total
        ]


def unpack(parts, chunks, cap, coarse):
    wide, _, rows, _ = parts[0].shape
    total = wide * cap
    steps = rows // 8 - 1
    out = pl.pallas_call(
        functools.partial(unpack_kernel, chunks, cap, coarse),
        out_shape=jax.ShapeDtypeStruct((coarse, coarse, total), F32),
        grid=(steps,),
        in_specs=[pl.BlockSpec(memory_space=pl.ANY)] * len(parts),
        out_specs=pl.BlockSpec((8, coarse, total), lambda s: (s, 0, 0)),
        scratch_shapes=[
            pltpu.VMEM((2, wide, cap, 8, LANES), F32),
            pltpu.VMEM((8 * LANES + 64, LANES), F32),
            pltpu.SemaphoreType.DMA((2,)),
            pltpu.SemaphoreType.DMA,
        ],
        cost_estimate=pl.CostEstimate(
            flops=0, bytes_accessed=total * 8 * rows * LANES, transcendentals=0
        ),
        name="unpack",
    )(*parts)
    return jnp.transpose(out, (2, 0, 1))


def local(face_blocks, face_elems, coarse_slot, prolong, fine_residual, block_inverse):
    wide = lax.axis_size("wide")
    narrow = lax.axis_size("narrow")
    devices = wide * narrow
    dev_rows = fine_residual.shape[0]
    owner_rows = dev_rows * narrow
    faces = face_blocks.shape[0]
    coarse = prolong.shape[1]
    cap = max(2, (2 * faces + wide - 1) // wide)
    first = max(1, cap // 5)
    chunks = (first, cap - first)
    rows_total = dev_rows * devices

    coarse_rhs = jnp.dot(fine_residual, prolong, precision=PRECISE)
    sweep_one = DAMPING * jnp.einsum("snm,sm->sn", block_inverse, coarse_rhs, precision=PRECISE)
    flat = dev_rows * coarse
    flat_pad = round_up(flat, 8 * LANES)
    packed = jnp.pad(sweep_one.reshape(-1), (0, flat_pad - flat)).reshape(1, flat_pad // LANES, LANES)
    spread = jnp.broadcast_to(packed, (devices,) + packed.shape[1:])
    gathered = lax.all_to_all(spread, BOTH, split_axis=0, concat_axis=0, tiled=True)

    fetch, valid, row_slot, col_slot = place_faces(
        face_elems, coarse_slot, owner_rows, cap, wide, chunks
    )
    rows_main = round_up(coarse, 8)
    p_pad = jnp.pad(prolong, ((0, 0), (0, 2 * LANES - coarse)))
    pt_pad = jnp.pad(prolong.T, ((0, rows_main - coarse), (0, 0)))
    parts, at = [], 0
    for ranks in chunks:
        n = wide * ranks
        packed_blocks = galerkin(
            face_blocks, p_pad, pt_pad, fetch[at : at + n], valid[at : at + n], wide, ranks
        )
        at += n
        parts.append(
            lax.all_to_all(packed_blocks, "wide", split_axis=0, concat_axis=0, tiled=True)
        )

    iterate = gathered.reshape(devices, flat_pad)[:, :flat].reshape(rows_total, coarse)
    vectors = jnp.take(iterate, col_slot, axis=0)
    fine_vectors = jnp.dot(vectors, prolong.T, precision=PRECISE)
    applied = jnp.einsum("fij,fj->fi", face_blocks, fine_vectors, precision=PRECISE)
    results = jnp.dot(applied, prolong, precision=PRECISE)
    selector = (
        lax.broadcasted_iota(jnp.int32, (rows_total, faces), 0) == row_slot[None, :]
    ).astype(F32)
    sums = jnp.dot(selector, results, precision=PRECISE).reshape(devices, flat)
    sums = jnp.pad(sums, ((0, 0), (0, flat_pad - flat))).reshape(devices, flat_pad // LANES, LANES)
    sums = lax.all_to_all(sums, BOTH, split_axis=0, concat_axis=0, tiled=True)
    coupling = jnp.sum(sums, axis=0).reshape(-1)[:flat].reshape(dev_rows, coarse)
    update = (1.0 - DAMPING) * coarse_rhs - coupling
    sweep_two = sweep_one + DAMPING * jnp.einsum(
        "snm,sm->sn", block_inverse, update, precision=PRECISE
    )
    correction = jnp.dot(sweep_two, prolong.T, precision=PRECISE)
    return (correction, unpack(parts, chunks, cap, coarse))


def solution(mesh):
    placed = (
        P(BOTH, None, None),
        P(BOTH, None),
        P(),
        P(),
        P(BOTH, None),
        P(BOTH, None, None),
    )
    return jax.shard_map(
        local,
        mesh=mesh,
        in_specs=placed,
        out_specs=(P(BOTH, None), P(BOTH, None, None)),
        check_vma=False,
    )
```

```python
import functools

import jax
import jax.numpy as jnp
from jax import lax
from jax.experimental import pallas as pl
from jax.experimental.pallas import tpu as pltpu
from jax.sharding import PartitionSpec as P

DAMPING = 0.7
PRECISE = lax.Precision.HIGHEST
BOTH = ("wide", "narrow")
LANES = 128
PAIR = 2
F32 = jnp.float32
BF16 = jnp.bfloat16


def round_up(value, unit):
    return (value + unit - 1) // unit * unit


def split(x):
    high = x.astype(BF16)
    return high, (x - high.astype(F32)).astype(BF16)


dot = functools.partial(jnp.dot, preferred_element_type=F32)


def send_plan(wide, cap):
    offsets = sorted(range(1, wide), key=lambda k: (-k.bit_length(), k))
    first = min(PAIR, cap)
    plan = [(offsets[0], 0, first)]
    if cap > first:
        plan.append((offsets[0], first, cap - first))
    return plan + [(k, 0, cap) for k in offsets[1:]]


def place_kernel(dev_rows, narrow, cap, elems, slots, me, pt, fetch, count, row, col, ph, pl_, th, tl, wide_pt):
    faces, wide = elems.shape[1], count.shape[0]
    owner_rows = dev_rows * narrow

    def clear(i, c):
        count[i] = 0
        return c

    def moved(r, owner):
        inner = r - owner * owner_rows
        n = lax.div(inner, dev_rows)
        return (n * wide + owner) * dev_rows + inner - n * dev_rows

    def put(f, c):
        r = slots[elems[0, f]]
        s = slots[elems[1, f]]
        owner = lax.div(r, owner_rows)
        row[f] = moved(r, owner)
        col[f] = moved(s, lax.div(s, owner_rows))
        at = owner ^ me[0]
        rank = count[at]
        count[at] = rank + 1
        fetch[at * cap + rank] = f
        return c

    def fill(k, c):
        for r in range(cap):

            @pl.when(r >= count[k])
            def _(r=r):
                fetch[k * cap + r] = fetch[k * cap + r - PAIR] if r >= PAIR else 0

        return c

    lax.fori_loop(0, wide, clear, 0)
    lax.fori_loop(0, faces, put, 0)
    lax.fori_loop(0, wide, fill, 0)
    rows, fine = th.shape
    wide_pt[...] = jnp.zeros_like(wide_pt)
    wide_pt[: pt.shape[0], :fine] = pt[...]
    th[...], tl[...] = split(wide_pt[:rows, :fine])
    ph[...], pl_[...] = split(wide_pt[...].T[:fine])


def place_faces(face_elems, coarse_slot, prolong, dev_rows, narrow, wide, cap):
    faces = face_elems.shape[0]
    fine, coarse = prolong.shape
    rows = round_up(coarse, 8)
    smem = pl.BlockSpec(memory_space=pltpu.SMEM)
    vmem = pl.BlockSpec(memory_space=pltpu.VMEM)
    ints = lambda n: jax.ShapeDtypeStruct((n,), jnp.int32)
    halves = lambda *s: jax.ShapeDtypeStruct(s, BF16)
    me = lax.axis_index("wide").astype(jnp.int32).reshape(1)
    return pl.pallas_call(
        functools.partial(place_kernel, dev_rows, narrow, cap),
        out_shape=(
            ints(wide * cap),
            ints(wide),
            ints(faces),
            ints(faces),
            halves(fine, 2 * LANES),
            halves(fine, 2 * LANES),
            halves(rows, fine),
            halves(rows, fine),
        ),
        in_specs=[smem, smem, smem, vmem],
        out_specs=(smem, smem, smem, smem, vmem, vmem, vmem, vmem),
        scratch_shapes=[pltpu.VMEM((2 * LANES, round_up(fine, LANES)), F32)],
        name="place_faces",
    )(face_elems.T, coarse_slot, me, prolong.T)


def galerkin_kernel(at, first, fetch, count, *refs):
    a_refs, (ph, pl_, th, tl, o_ref) = refs[:PAIR], refs[PAIR:]
    rank = first + pl.program_id(0) * PAIR
    rows = th.shape[0]
    full = ph.shape[0] // (2 * LANES) * 2 * LANES

    @pl.when(rank >= count[at])
    def _():
        o_ref[...] = jnp.zeros_like(o_ref)

    @pl.when(rank < count[at])
    def _():
        for j in range(PAIR):
            ah, al = split(a_refs[j][0])
            left = (ah[:, :full], al[:, :full], ah[:, :full], ah[:, full:], al[:, full:], ah[:, full:])
            right = (ph[:full], ph[:full], pl_[:full], ph[full:], ph[full:], pl_[full:])
            applied = dot(jnp.concatenate(left, axis=1), jnp.concatenate(right, axis=0))
            bh, bl = split(applied)
            block = dot(th[...], bh) + (dot(tl[...], bh) + dot(th[...], bl))
            if j:
                block = jnp.where(rank + j < count[at], block, 0.0)
            o_ref[j, :rows, :] = block[:, :LANES]
            rest = block[:, LANES:]
            turned = rest[:LANES].T[:8]
            corner = pltpu.roll(rest[LANES:rows], 0, 1, stride=8, stride_axis=0)
            corner = jnp.sum(corner, axis=0, keepdims=True)
            last = lax.broadcasted_iota(jnp.int32, (8, LANES), 0) == 7
            o_ref[j, rows:, :] = jnp.where(last, corner, turned)


def galerkin(face_blocks, operands, fetch, count, cap, piece):
    at, first, ranks = piece
    fine = face_blocks.shape[1]
    ph, _, th, _ = operands
    width, rows = ph.shape[1], th.shape[0]
    face = lambda j: lambda s, fetch, count: (fetch[at * cap + first + s * PAIR + j], 0, 0)
    const = lambda shape: pl.BlockSpec(shape, lambda s, fetch, count: (0, 0))
    return pl.pallas_call(
        functools.partial(galerkin_kernel, at, first),
        out_shape=jax.ShapeDtypeStruct((ranks, rows + 8, LANES), F32),
        grid_spec=pltpu.PrefetchScalarGridSpec(
            num_scalar_prefetch=2,
            grid=(ranks // PAIR,),
            in_specs=[pl.BlockSpec((1, fine, fine), face(j)) for j in range(PAIR)]
            + [const((fine, width))] * 2
            + [const((rows, fine))] * 2,
            out_specs=pl.BlockSpec((PAIR, rows + 8, LANES), lambda s, fetch, count: (s, 0, 0)),
        ),
        compiler_params=pltpu.CompilerParams(vmem_limit_bytes=50 << 20),
        cost_estimate=pl.CostEstimate(
            flops=ranks * 6 * fine * fine * width,
            bytes_accessed=ranks * 4 * (fine * fine + rows * LANES),
            transcendentals=0,
        ),
        name="galerkin",
    )(fetch, count, *[face_blocks] * PAIR, *operands)


def unpack_kernel(pieces, cap, coarse, me, *refs):
    parts, out = refs[: len(pieces)], refs[len(pieces)]
    buf, turned, sems = refs[len(pieces) + 1 :]
    step = pl.program_id(0)
    total, rows, _ = buf.shape
    main = rows - 8
    size = out.shape[0]
    groups = [(at, min(size, main - at)) for at in range(0, main, size)] + [(main, 8)]
    tail = len(groups) - 1

    def copies(g):
        at, extent = groups[g]
        for part, (offset, first, ranks) in zip(parts, pieces):
            ranks = min(ranks, cap - first)
            source = part.at[pl.ds(0, ranks), pl.ds(at, extent), :]
            target = buf.at[pl.ds((me[0] ^ offset) * cap + first, ranks), pl.ds(at, extent), :]
            yield pltpu.make_async_copy(source, target, sems.at[g])

    flat = buf.reshape(total * rows, LANES)

    def turn(r):
        x = flat[pl.ds(r, total, stride=rows), :]
        if total < LANES:
            x = jnp.concatenate([x, jnp.zeros((LANES - total, LANES), F32)], axis=0)
        return x.T

    @pl.when(step == 0)
    def _():
        for g in [tail, *range(tail)]:
            for copy in copies(g):
                copy.start()
        for copy in copies(tail):
            copy.wait()
        for k in range(7):
            turned[pl.ds(k, LANES, stride=8), :] = turn(main + k)
        turned[pl.ds(8 * LANES, 64), :] = turn(main + 7)[:64]

    for g in range(tail):

        @pl.when(step == g)
        def _(g=g):
            for copy in copies(g):
                copy.wait()

    for i in range(size):
        a = jnp.minimum(step * size + i, main - 1)
        out[i, :LANES, :] = turn(a)[:, :total]
        out[i, LANES:coarse, :] = turned[pl.ds(pl.multiple_of(a * 8, 8), 8), :][
            : coarse - LANES, :total
        ]


def unpack(parts, pieces, cap, coarse, wide, size=24):
    rows = parts[0].shape[1]
    total = wide * cap
    groups = pl.cdiv(rows - 8, size)
    me = lax.axis_index("wide").astype(jnp.int32).reshape(1)
    out = pl.pallas_call(
        functools.partial(unpack_kernel, pieces, cap, coarse),
        out_shape=jax.ShapeDtypeStruct((coarse, coarse, total), F32),
        grid=(groups,),
        in_specs=[pl.BlockSpec(memory_space=pltpu.SMEM)]
        + [pl.BlockSpec(memory_space=pl.ANY)] * len(parts),
        out_specs=pl.BlockSpec((size, coarse, total), lambda s: (s, 0, 0)),
        scratch_shapes=[
            pltpu.VMEM((total, rows, LANES), F32),
            pltpu.VMEM((8 * LANES + 64, LANES), F32),
            pltpu.SemaphoreType.DMA((groups + 1,)),
        ],
        compiler_params=pltpu.CompilerParams(vmem_limit_bytes=32 << 20),
        cost_estimate=pl.CostEstimate(
            flops=0, bytes_accessed=total * 8 * rows * LANES, transcendentals=0
        ),
        name="unpack",
    )(me, *parts)
    return jnp.transpose(out, (2, 0, 1))


def after(first, *values):
    out = lax.optimization_barrier((first, *values))
    return out[1:] if len(values) > 1 else out[1]


def everyone(x, axis, size):
    return lax.all_to_all(
        jnp.broadcast_to(x[None], (size, *x.shape)), axis, split_axis=0, concat_axis=0, tiled=True
    )


def local(face_blocks, face_elems, coarse_slot, prolong, fine_residual, block_inverse):
    wide = lax.axis_size("wide")
    narrow = lax.axis_size("narrow")
    dev_rows = fine_residual.shape[0]
    faces = face_blocks.shape[0]
    coarse = prolong.shape[1]
    cap = max(2, (2 * faces + wide - 1) // wide)
    slots = round_up(cap, PAIR)
    plan = send_plan(wide, slots)

    fetch, count, row, col, *operands = place_faces(
        face_elems, coarse_slot, prolong, dev_rows, narrow, wide, slots
    )
    parts, iterate = [], None
    for i, piece in enumerate(plan):
        block = galerkin(face_blocks, operands, fetch, count, slots, piece)
        fetch = after(block, fetch)
        pairs = [(w, w ^ piece[0]) for w in range(wide)]
        parts.append(lax.ppermute(block, "wide", pairs))
        if i == 1:
            fine_residual = after(block, fine_residual)
            rhs = jnp.dot(fine_residual, prolong, precision=PRECISE)
            sweep_one = DAMPING * jnp.einsum("snm,sm->sn", block_inverse, rhs, precision=PRECISE)
            fetch = after(sweep_one, fetch)
            iterate = everyone(sweep_one, "wide", wide)
    parts.append(galerkin(face_blocks, operands, fetch, count, slots, (0, 0, slots)))
    pieces = [*plan, (0, 0, slots)]
    iterate = after(parts[-1], iterate)
    iterate = everyone(iterate.reshape(wide * dev_rows, coarse), "narrow", narrow)
    iterate = iterate.reshape(-1, coarse)
    vectors = jnp.dot(jnp.take(iterate, col, axis=0), prolong.T, precision=PRECISE)
    applied = jnp.einsum("fij,fj->fi", face_blocks, vectors, precision=PRECISE)
    results = jnp.dot(applied, prolong, precision=PRECISE)
    total = iterate.shape[0]
    selector = (lax.broadcasted_iota(jnp.int32, (total, faces), 0) == row[None, :]).astype(F32)
    sums = jnp.dot(selector, results, precision=PRECISE).reshape(narrow, wide * dev_rows, coarse)
    sums = lax.all_to_all(sums, "narrow", split_axis=0, concat_axis=0, tiled=True)
    sums = jnp.sum(sums, axis=0).reshape(wide, dev_rows, coarse)
    sums = lax.all_to_all(sums, "wide", split_axis=0, concat_axis=0, tiled=True)
    coupling = jnp.sum(sums, axis=0)
    update = (1.0 - DAMPING) * rhs - coupling
    sweep_two = sweep_one + DAMPING * jnp.einsum(
        "snm,sm->sn", block_inverse, update, precision=PRECISE
    )
    correction = jnp.dot(sweep_two, prolong.T, precision=PRECISE)
    owned = unpack(parts, pieces, cap, coarse, wide)
    return (correction, owned)


def solution(mesh):
    placed = (
        P(BOTH, None, None),
        P(BOTH, None),
        P(),
        P(),
        P(BOTH, None),
        P(BOTH, None, None),
    )
    return jax.shard_map(
        local,
        mesh=mesh,
        in_specs=placed,
        out_specs=(P(BOTH, None), P(BOTH, None, None)),
        check_vma=False,
    )
```

```python
import functools

import jax
import jax.numpy as jnp
from jax import lax
from jax.experimental import pallas as pl
from jax.experimental.pallas import tpu as pltpu
from jax.sharding import PartitionSpec as P

DAMPING = 0.7
PRECISE = lax.Precision.HIGHEST
BOTH = ("wide", "narrow")
LANES = 128
PAIR = 2
EXCHANGE = 4
F32 = jnp.float32
BF16 = jnp.bfloat16


def round_up(value, unit):
    return (value + unit - 1) // unit * unit


def split(x):
    high = x.astype(BF16)
    return high, (x - high.astype(F32)).astype(BF16)


dot = functools.partial(jnp.dot, preferred_element_type=F32)


def send_plan(wide, cap):
    offsets = sorted(range(1, wide), key=lambda k: (-k.bit_length(), k))
    offsets = [k for k in offsets if 1 < k < wide - 1] + [wide - 1, 1]
    first = min(2 * PAIR, cap)
    plan = [(offsets[0], 0, first)]
    if cap > first:
        plan.append((offsets[0], first, cap - first))
    return plan + [(k, 0, cap) for k in offsets[1:]]


def place_kernel(owner_rows, cap, elems, slots, me, pt, fetch, count, ph, pl_, th, tl, p32, wide_pt):
    faces, wide = elems.shape[1], count.shape[0]

    def put(f, c):
        owner = lax.div(slots[elems[0, f]], owner_rows)
        at = owner ^ me[0]
        rank = count[at]
        count[at] = rank + 1
        fetch[at * cap + rank] = f
        return c

    for k in range(wide):
        count[k] = 0
    lax.fori_loop(0, faces, put, 0, unroll=8)

    def fill(k, c):
        for r in range(cap):

            @pl.when(r >= count[k])
            def _(r=r):
                fetch[k * cap + r] = fetch[k * cap + r - PAIR] if r >= PAIR else 0

        return c

    lax.fori_loop(0, wide, fill, 0)
    rows, fine = th.shape
    wide_pt[...] = jnp.zeros_like(wide_pt)
    wide_pt[: pt.shape[0], :fine] = pt[...]
    th[...], tl[...] = split(wide_pt[:rows, :fine])
    p32[...] = wide_pt[...].T[:fine]
    ph[...], pl_[...] = split(p32[...])


def index_kernel(dev_rows, narrow, wide, elems, slots, row, col):
    owner_rows = dev_rows * narrow

    def moved(r):
        owner = lax.div(r, owner_rows)
        inner = r - owner * owner_rows
        n = lax.div(inner, dev_rows)
        return (n * wide + owner) * dev_rows + inner - n * dev_rows

    def put(f, c):
        row[f] = moved(slots[elems[0, f]])
        col[f] = moved(slots[elems[1, f]])
        return c

    lax.fori_loop(0, elems.shape[1], put, 0, unroll=8)


SMEM = pl.BlockSpec(memory_space=pltpu.SMEM)
VMEM = pl.BlockSpec(memory_space=pltpu.VMEM)


def ints(n):
    return jax.ShapeDtypeStruct((n,), jnp.int32)


def place_faces(face_elems, coarse_slot, prolong, owner_rows, wide, cap):
    fine, coarse = prolong.shape
    rows = round_up(coarse, 8)
    halves = lambda *s: jax.ShapeDtypeStruct(s, BF16)
    me = lax.axis_index("wide").astype(jnp.int32).reshape(1)
    return pl.pallas_call(
        functools.partial(place_kernel, owner_rows, cap),
        out_shape=(
            ints(wide * cap),
            ints(wide),
            halves(fine, 2 * LANES),
            halves(fine, 2 * LANES),
            halves(rows, fine),
            halves(rows, fine),
            jax.ShapeDtypeStruct((fine, 2 * LANES), F32),
        ),
        in_specs=[SMEM, SMEM, SMEM, VMEM],
        out_specs=(SMEM, SMEM, VMEM, VMEM, VMEM, VMEM, VMEM),
        scratch_shapes=[pltpu.VMEM((2 * LANES, round_up(fine, LANES)), F32)],
        compiler_params=pltpu.CompilerParams(vmem_limit_bytes=8 << 20),
        name="place_faces",
    )(face_elems.T, coarse_slot, me, prolong.T)


def face_rows(face_elems, coarse_slot, dev_rows, narrow, wide):
    faces = face_elems.shape[0]
    return pl.pallas_call(
        functools.partial(index_kernel, dev_rows, narrow, wide),
        out_shape=(ints(faces), ints(faces)),
        in_specs=[SMEM, SMEM],
        out_specs=(SMEM, SMEM),
        compiler_params=pltpu.CompilerParams(vmem_limit_bytes=8 << 20),
        name="face_rows",
    )(face_elems.T, coarse_slot)


def product_kernel(a_ref, v_ref, p_ref, o_ref):
    for j in range(a_ref.shape[0]):
        applied = jnp.sum(a_ref[j] * v_ref[j : j + 1, :], axis=1, keepdims=True)
        o_ref[j : j + 1, :] = jnp.sum(p_ref[...] * applied, axis=0, keepdims=True)


def products(face_blocks, vectors, p32):
    faces, fine, _ = face_blocks.shape
    group = 8 if faces % 8 == 0 else faces
    width = p32.shape[1]
    return pl.pallas_call(
        product_kernel,
        out_shape=jax.ShapeDtypeStruct((faces, width), F32),
        grid=(faces // group,),
        in_specs=[
            pl.BlockSpec((group, fine, fine), lambda s: (s, 0, 0)),
            pl.BlockSpec((group, fine), lambda s: (s, 0)),
            VMEM,
        ],
        out_specs=pl.BlockSpec((group, width), lambda s: (s, 0)),
        compiler_params=pltpu.CompilerParams(vmem_limit_bytes=48 << 20),
        cost_estimate=pl.CostEstimate(
            flops=4 * faces * fine * fine, bytes_accessed=4 * faces * fine * fine, transcendentals=0
        ),
        name="products",
    )(face_blocks, vectors, p32)


def galerkin_kernel(at, first, fetch, count, *refs):
    a_refs, (ph, pl_, th, tl, o_ref) = refs[:PAIR], refs[PAIR:]
    rank = first + pl.program_id(0) * PAIR
    rows = th.shape[0]
    full = ph.shape[0] // (2 * LANES) * 2 * LANES

    @pl.when(rank >= count[at])
    def _():
        o_ref[...] = jnp.zeros_like(o_ref)

    @pl.when(rank < count[at])
    def _():
        left = []
        for j in range(PAIR):
            ah, al = split(a_refs[j][0])
            left.append(
                jnp.concatenate(
                    (ah[:, :full], al[:, :full], ah[:, :full], ah[:, full:], al[:, full:], ah[:, full:]),
                    axis=1,
                )
            )
        right = (ph[:full], ph[:full], pl_[:full], ph[full:], ph[full:], pl_[full:])
        applied = dot(jnp.concatenate(left, axis=0), jnp.concatenate(right, axis=0))
        fine = ph.shape[0]
        for j in range(PAIR):
            bh, bl = split(applied[j * fine : (j + 1) * fine])
            block = dot(th[...], bh) + (dot(tl[...], bh) + dot(th[...], bl))
            if j:
                block = jnp.where(rank + j < count[at], block, 0.0)
            o_ref[j, :rows, :] = block[:, :LANES]
            rest = block[:, LANES:]
            turned = rest[:LANES].T[:8]
            corner = pltpu.roll(rest[LANES:rows], 0, 1, stride=8, stride_axis=0)
            corner = jnp.sum(corner, axis=0, keepdims=True)
            last = lax.broadcasted_iota(jnp.int32, (8, LANES), 0) == 7
            o_ref[j, rows:, :] = jnp.where(last, corner, turned)


def galerkin(face_blocks, operands, fetch, count, cap, piece):
    at, first, ranks = piece
    fine = face_blocks.shape[1]
    ph, _, th, _ = operands
    width, rows = ph.shape[1], th.shape[0]
    face = lambda j: lambda s, fetch, count: (fetch[at * cap + first + s * PAIR + j], 0, 0)
    return pl.pallas_call(
        functools.partial(galerkin_kernel, at, first),
        out_shape=jax.ShapeDtypeStruct((ranks, rows + 8, LANES), F32),
        grid_spec=pltpu.PrefetchScalarGridSpec(
            num_scalar_prefetch=2,
            grid=(ranks // PAIR,),
            in_specs=[pl.BlockSpec((1, fine, fine), face(j)) for j in range(PAIR)]
            + [VMEM] * 4,
            out_specs=pl.BlockSpec((PAIR, rows + 8, LANES), lambda s, fetch, count: (s, 0, 0)),
        ),
        compiler_params=pltpu.CompilerParams(vmem_limit_bytes=50 << 20),
        cost_estimate=pl.CostEstimate(
            flops=ranks * 6 * fine * fine * width,
            bytes_accessed=ranks * 4 * (fine * fine + rows * LANES),
            transcendentals=0,
        ),
        name="galerkin",
    )(fetch, count, *[face_blocks] * PAIR, *operands)


def unpack_kernel(pieces, cap, coarse, me, *refs):
    parts, out = refs[: len(pieces)], refs[len(pieces)]
    buf, turned, sems = refs[len(pieces) + 1 :]
    step = pl.program_id(0)
    total, rows, _ = buf.shape
    main = rows - 8
    size = out.shape[0]
    groups = [(at, min(size, main - at)) for at in range(0, main, size)] + [(main, 8)]
    tail = len(groups) - 1

    def copies(g):
        at, extent = groups[g]
        for part, (offset, first, ranks) in zip(parts, pieces):
            ranks = min(ranks, cap - first)
            source = part.at[pl.ds(0, ranks), pl.ds(at, extent), :]
            target = buf.at[pl.ds((me[0] ^ offset) * cap + first, ranks), pl.ds(at, extent), :]
            yield pltpu.make_async_copy(source, target, sems.at[g])

    flat = buf.reshape(total * rows, LANES)

    def turn(r):
        x = flat[pl.ds(r, total, stride=rows), :]
        if total < LANES:
            x = jnp.concatenate([x, jnp.zeros((LANES - total, LANES), F32)], axis=0)
        return x.T

    @pl.when(step == 0)
    def _():
        for g in [tail, *range(tail)]:
            for copy in copies(g):
                copy.start()
        for copy in copies(tail):
            copy.wait()
        for k in range(7):
            turned[pl.ds(k, LANES, stride=8), :] = turn(main + k)
        turned[pl.ds(8 * LANES, 64), :] = turn(main + 7)[:64]

    for g in range(tail):

        @pl.when(step == g)
        def _(g=g):
            for copy in copies(g):
                copy.wait()

    for i in range(size):
        a = jnp.minimum(step * size + i, main - 1)
        out[i, :LANES, :] = turn(a)[:, :total]
        out[i, LANES:coarse, :] = turned[pl.ds(pl.multiple_of(a * 8, 8), 8), :][
            : coarse - LANES, :total
        ]


def unpack(parts, pieces, cap, coarse, wide, size=24):
    rows = parts[0].shape[1]
    total = wide * cap
    groups = pl.cdiv(rows - 8, size)
    me = lax.axis_index("wide").astype(jnp.int32).reshape(1)
    out = pl.pallas_call(
        functools.partial(unpack_kernel, pieces, cap, coarse),
        out_shape=jax.ShapeDtypeStruct((coarse, coarse, total), F32),
        grid=(groups,),
        in_specs=[pl.BlockSpec(memory_space=pltpu.SMEM)]
        + [pl.BlockSpec(memory_space=pl.ANY)] * len(parts),
        out_specs=pl.BlockSpec((size, coarse, total), lambda s: (s, 0, 0)),
        scratch_shapes=[
            pltpu.VMEM((total, rows, LANES), F32),
            pltpu.VMEM((8 * LANES + 64, LANES), F32),
            pltpu.SemaphoreType.DMA((groups + 1,)),
        ],
        compiler_params=pltpu.CompilerParams(vmem_limit_bytes=32 << 20),
        cost_estimate=pl.CostEstimate(
            flops=0, bytes_accessed=total * 8 * rows * LANES, transcendentals=0
        ),
        name="unpack",
    )(me, *parts)
    return jnp.transpose(out, (2, 0, 1))


def after(first, *values):
    out = lax.optimization_barrier((first, *values))
    return out[1:] if len(values) > 1 else out[1]


def everyone(x, axis, size):
    return lax.all_to_all(
        jnp.broadcast_to(x[None], (size, *x.shape)), axis, split_axis=0, concat_axis=0, tiled=True
    )


def local(face_blocks, face_elems, coarse_slot, prolong, fine_residual, block_inverse):
    wide = lax.axis_size("wide")
    narrow = lax.axis_size("narrow")
    dev_rows = fine_residual.shape[0]
    faces = face_blocks.shape[0]
    coarse = prolong.shape[1]
    cap = max(2, (2 * faces + wide - 1) // wide)
    slots = round_up(cap, PAIR)
    plan = send_plan(wide, slots)

    fetch, count, *operands, p32 = place_faces(
        face_elems, coarse_slot, prolong, dev_rows * narrow, wide, slots
    )
    parts = []
    for i, piece in enumerate(plan):
        block = galerkin(face_blocks, operands, fetch, count, slots, piece)
        fetch = after(block, fetch)
        pairs = [(w, w ^ piece[0]) for w in range(wide)]
        parts.append(lax.ppermute(block, "wide", pairs))
        if i == 0:
            fine_residual, face_elems = after(block, fine_residual, face_elems)
            rhs = jnp.dot(fine_residual, prolong, precision=PRECISE)
            sweep_one = DAMPING * jnp.einsum("snm,sm->sn", block_inverse, rhs, precision=PRECISE)
            fetch = after(sweep_one, fetch)
            iterate = everyone(sweep_one, "wide", wide)
        if i == EXCHANGE - 1:
            iterate, face_elems = after(block, iterate, face_elems)
            iterate = everyone(iterate.reshape(wide * dev_rows, coarse), "narrow", narrow)
            row, col = face_rows(face_elems, coarse_slot, dev_rows, narrow, wide)
            fetch = after(row, fetch)
        if i == EXCHANGE:
            iterate = after(block, iterate).reshape(-1, coarse)
            vectors = jnp.dot(jnp.take(iterate, col, axis=0), prolong.T, precision=PRECISE)
            results = products(face_blocks, vectors, p32)
            total = iterate.shape[0]
            selector = lax.broadcasted_iota(jnp.int32, (total, faces), 0) == row[None, :]
            sums = jnp.dot(selector.astype(F32), results, precision=PRECISE)[:, :coarse]
            sums = sums.reshape(narrow, wide * dev_rows, coarse)
            fetch = after(sums, fetch)
            sums = lax.all_to_all(sums, "narrow", split_axis=0, concat_axis=0, tiled=True)
        if i == EXCHANGE + 1:
            sums = jnp.sum(after(block, sums), axis=0).reshape(wide, dev_rows, coarse)
            fetch = after(sums, fetch)
            sums = lax.all_to_all(sums, "wide", split_axis=0, concat_axis=0, tiled=True)
    parts.append(galerkin(face_blocks, operands, fetch, count, slots, (0, 0, slots)))
    pieces = [*plan, (0, 0, slots)]
    coupling = jnp.sum(after(parts[-1], sums), axis=0)
    update = (1.0 - DAMPING) * rhs - coupling
    sweep_two = sweep_one + DAMPING * jnp.einsum(
        "snm,sm->sn", block_inverse, update, precision=PRECISE
    )
    correction = jnp.dot(sweep_two, prolong.T, precision=PRECISE)
    owned = unpack(parts, pieces, cap, coarse, wide)
    return (correction, owned)


def solution(mesh):
    placed = (
        P(BOTH, None, None),
        P(BOTH, None),
        P(),
        P(),
        P(BOTH, None),
        P(BOTH, None, None),
    )
    return jax.shard_map(
        local,
        mesh=mesh,
        in_specs=placed,
        out_specs=(P(BOTH, None), P(BOTH, None, None)),
        check_vma=False,
    )
```

```python
import functools

import jax
import jax.numpy as jnp
from jax import lax
from jax.experimental import pallas as pl
from jax.experimental.pallas import tpu as pltpu
from jax.sharding import PartitionSpec as P

DAMPING = 0.7
PRECISE = lax.Precision.HIGHEST
BOTH = ("wide", "narrow")
LANES = 128
PAIR = 2
EXCHANGE = 4
WHOLE_VMEM = 67043328
F32 = jnp.float32
BF16 = jnp.bfloat16


def round_up(value, unit):
    return (value + unit - 1) // unit * unit


def split(x):
    high = x.astype(BF16)
    return high, (x - high.astype(F32)).astype(BF16)


dot = functools.partial(jnp.dot, preferred_element_type=F32)


def send_plan(wide, cap):
    offsets = sorted(range(1, wide), key=lambda k: (-k.bit_length(), k))
    first = min(2 * PAIR, cap)
    plan = [(offsets[0], 0, first)]
    if cap > first:
        plan.append((offsets[0], first, cap - first))
    return plan + [(k, 0, cap) for k in offsets[1:]]


def place_kernel(
    owner_rows, cap, elems_in, slots_in, me, pt_in, fetch, count, ph, pl_, th, tl, p32, elems, slots, pt, wide_pt, sems
):
    faces, wide = elems.shape[1], count.shape[0]
    sources = ((elems_in, elems), (slots_in, slots), (pt_in, pt))
    copies = [pltpu.make_async_copy(a, b, sems.at[i]) for i, (a, b) in enumerate(sources)]
    for copy in copies:
        copy.start()
    wide_pt[...] = jnp.zeros_like(wide_pt)
    for copy in copies:
        copy.wait()

    def put(f, c):
        owner = lax.div(slots[elems[0, f]], owner_rows)
        at = owner ^ me[0]
        rank = count[at]
        count[at] = rank + 1
        fetch[at * cap + rank] = f
        return c

    for k in range(wide):
        count[k] = 0
    lax.fori_loop(0, faces, put, 0, unroll=8)

    def fill(k, c):
        for r in range(cap):

            @pl.when(r >= count[k])
            def _(r=r):
                fetch[k * cap + r] = fetch[k * cap + r - PAIR] if r >= PAIR else 0

        return c

    lax.fori_loop(0, wide, fill, 0)
    rows, fine = th.shape
    wide_pt[: pt.shape[0], :fine] = pt[...]
    th[...], tl[...] = split(wide_pt[:rows, :fine])
    p32[...] = wide_pt[...].T[:fine]
    ph[...], pl_[...] = split(p32[...])


def index_kernel(dev_rows, narrow, wide, elems, slots, row, col):
    owner_rows = dev_rows * narrow

    def moved(r):
        owner = lax.div(r, owner_rows)
        inner = r - owner * owner_rows
        n = lax.div(inner, dev_rows)
        return (n * wide + owner) * dev_rows + inner - n * dev_rows

    def put(f, c):
        row[f] = moved(slots[elems[0, f]])
        col[f] = moved(slots[elems[1, f]])
        return c

    lax.fori_loop(0, elems.shape[1], put, 0, unroll=8)


SMEM = pl.BlockSpec(memory_space=pltpu.SMEM)
VMEM = pl.BlockSpec(memory_space=pltpu.VMEM)
HBM = pl.BlockSpec(memory_space=pltpu.HBM)


def ints(n):
    return jax.ShapeDtypeStruct((n,), jnp.int32)


def place_faces(face_elems, coarse_slot, prolong, owner_rows, wide, cap):
    fine, coarse = prolong.shape
    rows = round_up(coarse, 8)
    halves = lambda *s: jax.ShapeDtypeStruct(s, BF16)
    me = lax.axis_index("wide").astype(jnp.int32).reshape(1)
    return pl.pallas_call(
        functools.partial(place_kernel, owner_rows, cap),
        out_shape=(
            ints(wide * cap),
            ints(wide),
            halves(fine, 2 * LANES),
            halves(fine, 2 * LANES),
            halves(rows, fine),
            halves(rows, fine),
            jax.ShapeDtypeStruct((fine, 2 * LANES), F32),
        ),
        in_specs=[HBM, HBM, SMEM, HBM],
        out_specs=(SMEM, SMEM, VMEM, VMEM, VMEM, VMEM, VMEM),
        scratch_shapes=[
            pltpu.SMEM(face_elems.shape[::-1], jnp.int32),
            pltpu.SMEM(coarse_slot.shape, jnp.int32),
            pltpu.VMEM((coarse, fine), F32),
            pltpu.VMEM((2 * LANES, round_up(fine, LANES)), F32),
            pltpu.SemaphoreType.DMA((3,)),
        ],
        compiler_params=pltpu.CompilerParams(vmem_limit_bytes=WHOLE_VMEM),
        name="place_faces",
    )(face_elems.T, coarse_slot, me, prolong.T)


def face_rows(face_elems, coarse_slot, dev_rows, narrow, wide):
    faces = face_elems.shape[0]
    return pl.pallas_call(
        functools.partial(index_kernel, dev_rows, narrow, wide),
        out_shape=(ints(faces), ints(faces)),
        in_specs=[SMEM, SMEM],
        out_specs=(SMEM, SMEM),
        compiler_params=pltpu.CompilerParams(vmem_limit_bytes=8 << 20),
        name="face_rows",
    )(face_elems.T, coarse_slot)


def apply_blocks(blocks, vectors):
    coarse = blocks.shape[0]
    lane = lax.broadcasted_iota(jnp.int32, vectors.shape, 1)

    def add(n, out):
        value = jnp.sum(blocks[n] * vectors, axis=1, keepdims=True)
        return jnp.where(lane == n, value, out)

    return lax.fori_loop(0, coarse, add, jnp.zeros_like(vectors), unroll=9)


def sweep_one_kernel(residual, p32, blocks, rhs, sweep):
    rhs[...] = jnp.dot(residual[...], p32[...], precision=PRECISE, preferred_element_type=F32)
    sweep[...] = DAMPING * apply_blocks(blocks, rhs[:, : blocks.shape[0]])


def sweep_one_of(residual, p32, blocks):
    rows, coarse = residual.shape[0], blocks.shape[0]
    return pl.pallas_call(
        sweep_one_kernel,
        out_shape=(
            jax.ShapeDtypeStruct((rows, p32.shape[1]), F32),
            jax.ShapeDtypeStruct((rows, coarse), F32),
        ),
        in_specs=[VMEM] * 3,
        out_specs=(VMEM, VMEM),
        compiler_params=pltpu.CompilerParams(vmem_limit_bytes=8 << 20),
        name="sweep_one",
    )(residual, p32, blocks)


def sweep_two_kernel(sums, rhs, sweep, pt, blocks, out):
    coarse = blocks.shape[0]
    update = (1.0 - DAMPING) * rhs[:, :coarse] - jnp.sum(sums[...], axis=0)
    last = sweep[...] + DAMPING * apply_blocks(blocks, update)
    out[...] = jnp.dot(last, pt[...], precision=PRECISE, preferred_element_type=F32)


def sweep_two_of(sums, rhs, sweep, pt, blocks):
    return pl.pallas_call(
        sweep_two_kernel,
        out_shape=jax.ShapeDtypeStruct((rhs.shape[0], pt.shape[1]), F32),
        in_specs=[VMEM] * 5,
        out_specs=VMEM,
        compiler_params=pltpu.CompilerParams(vmem_limit_bytes=8 << 20),
        name="sweep_two",
    )(sums, rhs, sweep, pt, blocks)


def product_kernel(a_ref, v_ref, p_ref, o_ref):
    for j in range(a_ref.shape[0]):
        applied = jnp.sum(a_ref[j] * v_ref[j : j + 1, :], axis=1, keepdims=True)
        o_ref[j : j + 1, :] = jnp.sum(p_ref[...] * applied, axis=0, keepdims=True)


def products(face_blocks, vectors, p32):
    faces, fine, _ = face_blocks.shape
    group = 8 if faces % 8 == 0 else faces
    width = p32.shape[1]
    return pl.pallas_call(
        product_kernel,
        out_shape=jax.ShapeDtypeStruct((faces, width), F32),
        grid=(faces // group,),
        in_specs=[
            pl.BlockSpec((group, fine, fine), lambda s: (s, 0, 0)),
            pl.BlockSpec((group, fine), lambda s: (s, 0)),
            VMEM,
        ],
        out_specs=pl.BlockSpec((group, width), lambda s: (s, 0)),
        compiler_params=pltpu.CompilerParams(vmem_limit_bytes=48 << 20),
        cost_estimate=pl.CostEstimate(
            flops=4 * faces * fine * fine, bytes_accessed=4 * faces * fine * fine, transcendentals=0
        ),
        name="products",
    )(face_blocks, vectors, p32)


def galerkin_kernel(at, first, fetch, count, *refs):
    a_refs, (ph, pl_, th, tl, o_ref) = refs[:PAIR], refs[PAIR:]
    rank = first + pl.program_id(0) * PAIR
    rows = th.shape[0]
    full = ph.shape[0] // (2 * LANES) * 2 * LANES

    @pl.when(rank >= count[at])
    def _():
        o_ref[...] = jnp.zeros_like(o_ref)

    @pl.when(rank < count[at])
    def _():
        left = []
        for j in range(PAIR):
            ah, al = split(a_refs[j][0])
            left.append(
                jnp.concatenate(
                    (ah[:, :full], al[:, :full], ah[:, :full], ah[:, full:], al[:, full:], ah[:, full:]),
                    axis=1,
                )
            )
        right = (ph[:full], ph[:full], pl_[:full], ph[full:], ph[full:], pl_[full:])
        applied = dot(jnp.concatenate(left, axis=0), jnp.concatenate(right, axis=0))
        fine = ph.shape[0]
        for j in range(PAIR):
            bh, bl = split(applied[j * fine : (j + 1) * fine])
            block = dot(th[...], bh) + (dot(tl[...], bh) + dot(th[...], bl))
            if j:
                block = jnp.where(rank + j < count[at], block, 0.0)
            o_ref[j, :rows, :] = block[:, :LANES]
            rest = block[:, LANES:]
            turned = rest[:LANES].T[:8]
            corner = pltpu.roll(rest[LANES:rows], 0, 1, stride=8, stride_axis=0)
            corner = jnp.sum(corner, axis=0, keepdims=True)
            last = lax.broadcasted_iota(jnp.int32, (8, LANES), 0) == 7
            o_ref[j, rows:, :] = jnp.where(last, corner, turned)


def galerkin(face_blocks, operands, fetch, count, cap, piece, grant=50 << 20):
    at, first, ranks = piece
    fine = face_blocks.shape[1]
    ph, _, th, _ = operands
    width, rows = ph.shape[1], th.shape[0]
    face = lambda j: lambda s, fetch, count: (fetch[at * cap + first + s * PAIR + j], 0, 0)
    return pl.pallas_call(
        functools.partial(galerkin_kernel, at, first),
        out_shape=jax.ShapeDtypeStruct((ranks, rows + 8, LANES), F32),
        grid_spec=pltpu.PrefetchScalarGridSpec(
            num_scalar_prefetch=2,
            grid=(ranks // PAIR,),
            in_specs=[pl.BlockSpec((1, fine, fine), face(j)) for j in range(PAIR)]
            + [VMEM] * 4,
            out_specs=pl.BlockSpec((PAIR, rows + 8, LANES), lambda s, fetch, count: (s, 0, 0)),
        ),
        compiler_params=pltpu.CompilerParams(vmem_limit_bytes=grant),
        cost_estimate=pl.CostEstimate(
            flops=ranks * 6 * fine * fine * width,
            bytes_accessed=ranks * 4 * (fine * fine + rows * LANES),
            transcendentals=0,
        ),
        name="galerkin",
    )(fetch, count, *[face_blocks] * PAIR, *operands)


def unpack_kernel(pieces, cap, coarse, me, *refs):
    parts, out = refs[: len(pieces)], refs[len(pieces)]
    buf, turned, sems = refs[len(pieces) + 1 :]
    step = pl.program_id(0)
    total, rows, _ = buf.shape
    main = rows - 8
    size = out.shape[0]
    groups = [(at, min(size, main - at)) for at in range(0, main, size)] + [(main, 8)]
    tail = len(groups) - 1

    def copies(g):
        at, extent = groups[g]
        for part, (offset, first, ranks) in zip(parts, pieces):
            ranks = min(ranks, cap - first)
            source = part.at[pl.ds(0, ranks), pl.ds(at, extent), :]
            target = buf.at[pl.ds((me[0] ^ offset) * cap + first, ranks), pl.ds(at, extent), :]
            yield pltpu.make_async_copy(source, target, sems.at[g])

    flat = buf.reshape(total * rows, LANES)

    def turn(r):
        x = flat[pl.ds(r, total, stride=rows), :]
        if total < LANES:
            x = jnp.concatenate([x, jnp.zeros((LANES - total, LANES), F32)], axis=0)
        return x.T

    @pl.when(step == 0)
    def _():
        for g in [tail, *range(tail)]:
            for copy in copies(g):
                copy.start()
        for copy in copies(tail):
            copy.wait()
        for k in range(7):
            turned[pl.ds(k, LANES, stride=8), :] = turn(main + k)
        turned[pl.ds(8 * LANES, 64), :] = turn(main + 7)[:64]

    for g in range(tail):

        @pl.when(step == g)
        def _(g=g):
            for copy in copies(g):
                copy.wait()

    for i in range(size):
        a = jnp.minimum(step * size + i, main - 1)
        out[i, :LANES, :] = turn(a)[:, :total]
        out[i, LANES:coarse, :] = turned[pl.ds(pl.multiple_of(a * 8, 8), 8), :][
            : coarse - LANES, :total
        ]


def unpack(parts, pieces, cap, coarse, wide, size=24):
    rows = parts[0].shape[1]
    total = wide * cap
    groups = pl.cdiv(rows - 8, size)
    me = lax.axis_index("wide").astype(jnp.int32).reshape(1)
    out = pl.pallas_call(
        functools.partial(unpack_kernel, pieces, cap, coarse),
        out_shape=jax.ShapeDtypeStruct((coarse, coarse, total), F32),
        grid=(groups,),
        in_specs=[pl.BlockSpec(memory_space=pltpu.SMEM)]
        + [pl.BlockSpec(memory_space=pl.ANY)] * len(parts),
        out_specs=pl.BlockSpec((size, coarse, total), lambda s: (s, 0, 0)),
        scratch_shapes=[
            pltpu.VMEM((total, rows, LANES), F32),
            pltpu.VMEM((8 * LANES + 64, LANES), F32),
            pltpu.SemaphoreType.DMA((groups + 1,)),
        ],
        compiler_params=pltpu.CompilerParams(vmem_limit_bytes=32 << 20),
        cost_estimate=pl.CostEstimate(
            flops=0, bytes_accessed=total * 8 * rows * LANES, transcendentals=0
        ),
        name="unpack",
    )(me, *parts)
    return jnp.transpose(out, (2, 0, 1))


def after(first, *values):
    out = lax.optimization_barrier((first, *values))
    return out[1:] if len(values) > 1 else out[1]


def everyone(x, axis, size):
    return lax.all_to_all(
        jnp.broadcast_to(x[None], (size, *x.shape)), axis, split_axis=0, concat_axis=0, tiled=True
    )


def local(face_blocks, face_elems, coarse_slot, prolong, fine_residual, block_inverse):
    wide = lax.axis_size("wide")
    narrow = lax.axis_size("narrow")
    dev_rows = fine_residual.shape[0]
    faces = face_blocks.shape[0]
    coarse = prolong.shape[1]
    cap = max(2, (2 * faces + wide - 1) // wide)
    slots = round_up(cap, PAIR)
    plan = send_plan(wide, slots)

    fetch, count, *operands, p32 = place_faces(
        face_elems, coarse_slot, prolong, dev_rows * narrow, wide, slots
    )
    parts = []
    for i, piece in enumerate(plan):
        grant = 50 << 20 if i else WHOLE_VMEM
        block = galerkin(face_blocks, operands, fetch, count, slots, piece, grant)
        fetch = after(block, fetch)
        pairs = [(w, w ^ piece[0]) for w in range(wide)]
        parts.append(lax.ppermute(block, "wide", pairs))
        if i == 0:
            fine_residual, face_elems = after(block, fine_residual, face_elems)
            inverse = jnp.transpose(block_inverse, (1, 0, 2))
            rhs, sweep_one = sweep_one_of(fine_residual, p32, inverse)
            fetch = after(sweep_one, fetch)
            iterate = everyone(sweep_one, "wide", wide)
        if i == EXCHANGE - 1:
            iterate, face_elems = after(block, iterate, face_elems)
            iterate = everyone(iterate.reshape(wide * dev_rows, coarse), "narrow", narrow)
            row, col = face_rows(face_elems, coarse_slot, dev_rows, narrow, wide)
            fetch = after(row, fetch)
        if i == EXCHANGE + 1:
            iterate = after(block, iterate).reshape(-1, coarse)
            vectors = jnp.dot(jnp.take(iterate, col, axis=0), prolong.T, precision=PRECISE)
            results = products(face_blocks, vectors, p32)
            total = iterate.shape[0]
            selector = lax.broadcasted_iota(jnp.int32, (total, faces), 0) == row[None, :]
            sums = jnp.dot(selector.astype(F32), results, precision=PRECISE)[:, :coarse]
            sums = sums.reshape(narrow, wide * dev_rows, coarse)
            fetch = after(sums, fetch)
            sums = lax.all_to_all(sums, "narrow", split_axis=0, concat_axis=0, tiled=True)
        if i == len(plan) - 1:
            sums = jnp.sum(after(block, sums), axis=0).reshape(wide, dev_rows, coarse)
            fetch = after(sums, fetch)
            sums = lax.all_to_all(sums, "wide", split_axis=0, concat_axis=0, tiled=True)
    parts.append(galerkin(face_blocks, operands, fetch, count, slots, (0, 0, slots)))
    pieces = [*plan, (0, 0, slots)]
    sums = after(parts[-1], sums)
    correction = sweep_two_of(sums, rhs, sweep_one, prolong.T, inverse)
    owned = unpack(parts, pieces, cap, coarse, wide)
    return (correction, owned)


def solution(mesh):
    placed = (
        P(BOTH, None, None),
        P(BOTH, None),
        P(),
        P(),
        P(BOTH, None),
        P(BOTH, None, None),
    )
    return jax.shard_map(
        local,
        mesh=mesh,
        in_specs=placed,
        out_specs=(P(BOTH, None), P(BOTH, None, None)),
        check_vma=False,
    )
```

```python
import functools

import jax
import jax.numpy as jnp
from jax import lax
from jax.experimental import pallas as pl
from jax.experimental.pallas import tpu as pltpu
from jax.sharding import PartitionSpec as P

DAMPING = 0.7
PRECISE = lax.Precision.HIGHEST
BOTH = ("wide", "narrow")
LANES = 128
PAIR = 2
WHOLE_VMEM = 67043328
F32 = jnp.float32
BF16 = jnp.bfloat16


def round_up(value, unit):
    return (value + unit - 1) // unit * unit


def split(x):
    high = x.astype(BF16)
    return high, (x - high.astype(F32)).astype(BF16)


dot = functools.partial(jnp.dot, preferred_element_type=F32)


def send_plan(wide, cap):
    offsets = sorted(range(1, wide), key=lambda k: (-k.bit_length(), k))
    first = min(3 * PAIR, cap)
    plan = [(offsets[0], 0, first)]
    if cap > first:
        plan.append((offsets[0], first, cap - first))
    return plan + [(k, 0, cap) for k in offsets[1:]]


def place_kernel(
    owner_rows, cap, elems_in, slots_in, me, pt_in, fetch, count, ph, pl_, th, tl, p32, elems, slots, pt, wide_pt, sems
):
    faces, wide = elems.shape[1], count.shape[0]
    sources = ((elems_in, elems), (slots_in, slots), (pt_in, pt))
    copies = [pltpu.make_async_copy(a, b, sems.at[i]) for i, (a, b) in enumerate(sources)]
    for copy in copies:
        copy.start()
    wide_pt[...] = jnp.zeros_like(wide_pt)
    for copy in copies:
        copy.wait()

    def put(f, c):
        owner = lax.div(slots[elems[0, f]], owner_rows)
        at = owner ^ me[0]
        rank = count[at]
        count[at] = rank + 1
        fetch[at * cap + rank] = f
        return c

    for k in range(wide):
        count[k] = 0
    lax.fori_loop(0, faces, put, 0, unroll=8)

    def fill(k, c):
        for r in range(cap):

            @pl.when(r >= count[k])
            def _(r=r):
                fetch[k * cap + r] = fetch[k * cap + r - PAIR] if r >= PAIR else 0

        return c

    lax.fori_loop(0, wide, fill, 0)
    rows, fine = th.shape
    wide_pt[: pt.shape[0], :fine] = pt[...]
    th[...], tl[...] = split(wide_pt[:rows, :fine])
    p32[...] = wide_pt[...].T[:fine]
    ph[...], pl_[...] = split(p32[...])


def index_kernel(dev_rows, narrow, wide, elems, slots, row, col):
    owner_rows = dev_rows * narrow

    def moved(r):
        owner = lax.div(r, owner_rows)
        inner = r - owner * owner_rows
        n = lax.div(inner, dev_rows)
        return (n * wide + owner) * dev_rows + inner - n * dev_rows

    def put(f, c):
        row[f] = moved(slots[elems[0, f]])
        col[f] = moved(slots[elems[1, f]])
        return c

    lax.fori_loop(0, elems.shape[1], put, 0, unroll=8)


SMEM = pl.BlockSpec(memory_space=pltpu.SMEM)
VMEM = pl.BlockSpec(memory_space=pltpu.VMEM)
HBM = pl.BlockSpec(memory_space=pltpu.HBM)


def ints(n):
    return jax.ShapeDtypeStruct((n,), jnp.int32)


def place_faces(face_elems, coarse_slot, prolong, owner_rows, wide, cap):
    fine, coarse = prolong.shape
    rows = round_up(coarse, 8)
    halves = lambda *s: jax.ShapeDtypeStruct(s, BF16)
    me = lax.axis_index("wide").astype(jnp.int32).reshape(1)
    return pl.pallas_call(
        functools.partial(place_kernel, owner_rows, cap),
        out_shape=(
            ints(wide * cap),
            ints(wide),
            halves(fine, 2 * LANES),
            halves(fine, 2 * LANES),
            halves(rows, fine),
            halves(rows, fine),
            jax.ShapeDtypeStruct((fine, 2 * LANES), F32),
        ),
        in_specs=[HBM, HBM, SMEM, HBM],
        out_specs=(SMEM, SMEM, VMEM, VMEM, VMEM, VMEM, VMEM),
        scratch_shapes=[
            pltpu.SMEM(face_elems.shape[::-1], jnp.int32),
            pltpu.SMEM(coarse_slot.shape, jnp.int32),
            pltpu.VMEM((coarse, fine), F32),
            pltpu.VMEM((2 * LANES, round_up(fine, LANES)), F32),
            pltpu.SemaphoreType.DMA((3,)),
        ],
        compiler_params=pltpu.CompilerParams(vmem_limit_bytes=WHOLE_VMEM),
        name="place_faces",
    )(face_elems.T, coarse_slot, me, prolong.T)


def face_rows(face_elems, coarse_slot, dev_rows, narrow, wide):
    faces = face_elems.shape[0]
    return pl.pallas_call(
        functools.partial(index_kernel, dev_rows, narrow, wide),
        out_shape=(ints(faces), ints(faces)),
        in_specs=[SMEM, SMEM],
        out_specs=(SMEM, SMEM),
        compiler_params=pltpu.CompilerParams(vmem_limit_bytes=8 << 20),
        name="face_rows",
    )(face_elems.T, coarse_slot)


def apply_blocks(blocks, vectors):
    coarse = blocks.shape[0]
    lane = lax.broadcasted_iota(jnp.int32, vectors.shape, 1)

    def add(n, out):
        value = jnp.sum(blocks[n] * vectors, axis=1, keepdims=True)
        return jnp.where(lane == n, value, out)

    return lax.fori_loop(0, coarse, add, jnp.zeros_like(vectors), unroll=9)


def sweep_one_kernel(residual, p32, blocks, rhs, sweep, copies):
    rhs[...] = jnp.dot(residual[...], p32[...], precision=PRECISE, preferred_element_type=F32)
    sweep[...] = DAMPING * apply_blocks(blocks, rhs[:, : blocks.shape[0]])
    copies[...] = jnp.broadcast_to(sweep[...][None], copies.shape)


def sweep_one_of(residual, p32, blocks, wide):
    rows, coarse = residual.shape[0], blocks.shape[0]
    return pl.pallas_call(
        sweep_one_kernel,
        out_shape=(
            jax.ShapeDtypeStruct((rows, p32.shape[1]), F32),
            jax.ShapeDtypeStruct((rows, coarse), F32),
            jax.ShapeDtypeStruct((wide, rows, coarse), F32),
        ),
        in_specs=[VMEM] * 3,
        out_specs=(VMEM, VMEM, VMEM),
        compiler_params=pltpu.CompilerParams(vmem_limit_bytes=WHOLE_VMEM),
        name="sweep_one",
    )(residual, p32, blocks)


def sweep_two_kernel(sums, rhs, sweep, pt, blocks, out):
    coarse = blocks.shape[0]
    update = (1.0 - DAMPING) * rhs[:, :coarse] - jnp.sum(sums[...], axis=0)
    last = sweep[...] + DAMPING * apply_blocks(blocks, update)
    out[...] = jnp.dot(last, pt[...], precision=PRECISE, preferred_element_type=F32)


def sweep_two_of(sums, rhs, sweep, pt, blocks):
    return pl.pallas_call(
        sweep_two_kernel,
        out_shape=jax.ShapeDtypeStruct((rhs.shape[0], pt.shape[1]), F32),
        in_specs=[VMEM] * 5,
        out_specs=VMEM,
        compiler_params=pltpu.CompilerParams(vmem_limit_bytes=8 << 20),
        name="sweep_two",
    )(sums, rhs, sweep, pt, blocks)


def product_kernel(a_ref, v_ref, p_ref, o_ref):
    for j in range(a_ref.shape[0]):
        applied = jnp.sum(a_ref[j] * v_ref[j : j + 1, :], axis=1, keepdims=True)
        o_ref[j : j + 1, :] = jnp.sum(p_ref[...] * applied, axis=0, keepdims=True)


def products(face_blocks, vectors, p32):
    faces, fine, _ = face_blocks.shape
    group = 8 if faces % 8 == 0 else faces
    width = p32.shape[1]
    return pl.pallas_call(
        product_kernel,
        out_shape=jax.ShapeDtypeStruct((faces, width), F32),
        grid=(faces // group,),
        in_specs=[
            pl.BlockSpec((group, fine, fine), lambda s: (s, 0, 0)),
            pl.BlockSpec((group, fine), lambda s: (s, 0)),
            VMEM,
        ],
        out_specs=pl.BlockSpec((group, width), lambda s: (s, 0)),
        compiler_params=pltpu.CompilerParams(vmem_limit_bytes=48 << 20),
        cost_estimate=pl.CostEstimate(
            flops=4 * faces * fine * fine, bytes_accessed=4 * faces * fine * fine, transcendentals=0
        ),
        name="products",
    )(face_blocks, vectors, p32)


def galerkin_kernel(at, first, fetch, count, *refs):
    a_refs, (ph, pl_, th, tl, o_ref) = refs[:PAIR], refs[PAIR:]
    rank = first + pl.program_id(0) * PAIR
    rows = th.shape[0]
    full = ph.shape[0] // (2 * LANES) * 2 * LANES

    @pl.when(rank >= count[at])
    def _():
        o_ref[...] = jnp.zeros_like(o_ref)

    @pl.when(rank < count[at])
    def _():
        left = []
        for j in range(PAIR):
            ah, al = split(a_refs[j][0])
            left.append(
                jnp.concatenate(
                    (ah[:, :full], al[:, :full], ah[:, :full], ah[:, full:], al[:, full:], ah[:, full:]),
                    axis=1,
                )
            )
        right = (ph[:full], ph[:full], pl_[:full], ph[full:], ph[full:], pl_[full:])
        applied = dot(jnp.concatenate(left, axis=0), jnp.concatenate(right, axis=0))
        fine = ph.shape[0]
        for j in range(PAIR):
            bh, bl = split(applied[j * fine : (j + 1) * fine])
            block = dot(th[...], bh) + (dot(tl[...], bh) + dot(th[...], bl))
            if j:
                block = jnp.where(rank + j < count[at], block, 0.0)
            o_ref[j, :rows, :] = block[:, :LANES]
            rest = block[:, LANES:]
            turned = rest[:LANES].T[:8]
            corner = pltpu.roll(rest[LANES:rows], 0, 1, stride=8, stride_axis=0)
            corner = jnp.sum(corner, axis=0, keepdims=True)
            last = lax.broadcasted_iota(jnp.int32, (8, LANES), 0) == 7
            o_ref[j, rows:, :] = jnp.where(last, corner, turned)


def galerkin(face_blocks, operands, fetch, count, cap, piece):
    at, first, ranks = piece
    fine = face_blocks.shape[1]
    ph, _, th, _ = operands
    width, rows = ph.shape[1], th.shape[0]
    face = lambda j: lambda s, fetch, count: (fetch[at * cap + first + s * PAIR + j], 0, 0)
    return pl.pallas_call(
        functools.partial(galerkin_kernel, at, first),
        out_shape=jax.ShapeDtypeStruct((ranks, rows + 8, LANES), F32),
        grid_spec=pltpu.PrefetchScalarGridSpec(
            num_scalar_prefetch=2,
            grid=(ranks // PAIR,),
            in_specs=[pl.BlockSpec((1, fine, fine), face(j)) for j in range(PAIR)]
            + [VMEM] * 4,
            out_specs=pl.BlockSpec((PAIR, rows + 8, LANES), lambda s, fetch, count: (s, 0, 0)),
        ),
        compiler_params=pltpu.CompilerParams(vmem_limit_bytes=WHOLE_VMEM),
        cost_estimate=pl.CostEstimate(
            flops=ranks * 6 * fine * fine * width,
            bytes_accessed=ranks * 4 * (fine * fine + rows * LANES),
            transcendentals=0,
        ),
        name="galerkin",
    )(fetch, count, *[face_blocks] * PAIR, *operands)


def unpack_kernel(pieces, cap, coarse, me, *refs):
    parts, out = refs[: len(pieces)], refs[len(pieces)]
    buf, turned, sems = refs[len(pieces) + 1 :]
    step = pl.program_id(0)
    total, rows, _ = buf.shape
    main = rows - 8
    size = out.shape[0]
    groups = [(at, min(size, main - at)) for at in range(0, main, size)] + [(main, 8)]
    tail = len(groups) - 1

    def copies(g):
        at, extent = groups[g]
        for part, (offset, first, ranks) in zip(parts, pieces):
            ranks = min(ranks, cap - first)
            source = part.at[pl.ds(0, ranks), pl.ds(at, extent), :]
            target = buf.at[pl.ds((me[0] ^ offset) * cap + first, ranks), pl.ds(at, extent), :]
            yield pltpu.make_async_copy(source, target, sems.at[g])

    flat = buf.reshape(total * rows, LANES)

    def turn(r):
        x = flat[pl.ds(r, total, stride=rows), :]
        if total < LANES:
            x = jnp.concatenate([x, jnp.zeros((LANES - total, LANES), F32)], axis=0)
        return x.T

    @pl.when(step == 0)
    def _():
        for g in [tail, *range(tail)]:
            for copy in copies(g):
                copy.start()
        for copy in copies(tail):
            copy.wait()
        for k in range(7):
            turned[pl.ds(k, LANES, stride=8), :] = turn(main + k)
        turned[pl.ds(8 * LANES, 64), :] = turn(main + 7)[:64]

    for g in range(tail):

        @pl.when(step == g)
        def _(g=g):
            for copy in copies(g):
                copy.wait()

    for i in range(size):
        a = jnp.minimum(step * size + i, main - 1)
        out[i, :LANES, :] = turn(a)[:, :total]
        out[i, LANES:coarse, :] = turned[pl.ds(pl.multiple_of(a * 8, 8), 8), :][
            : coarse - LANES, :total
        ]


def unpack(parts, pieces, cap, coarse, wide, size=24):
    rows = parts[0].shape[1]
    total = wide * cap
    groups = pl.cdiv(rows - 8, size)
    me = lax.axis_index("wide").astype(jnp.int32).reshape(1)
    out = pl.pallas_call(
        functools.partial(unpack_kernel, pieces, cap, coarse),
        out_shape=jax.ShapeDtypeStruct((coarse, coarse, total), F32),
        grid=(groups,),
        in_specs=[pl.BlockSpec(memory_space=pltpu.SMEM)]
        + [pl.BlockSpec(memory_space=pl.ANY)] * len(parts),
        out_specs=pl.BlockSpec((size, coarse, total), lambda s: (s, 0, 0)),
        scratch_shapes=[
            pltpu.VMEM((total, rows, LANES), F32),
            pltpu.VMEM((8 * LANES + 64, LANES), F32),
            pltpu.SemaphoreType.DMA((groups + 1,)),
        ],
        compiler_params=pltpu.CompilerParams(vmem_limit_bytes=32 << 20),
        cost_estimate=pl.CostEstimate(
            flops=0, bytes_accessed=total * 8 * rows * LANES, transcendentals=0
        ),
        name="unpack",
    )(me, *parts)
    return jnp.transpose(out, (2, 0, 1))


def after(first, *values):
    out = lax.optimization_barrier((first, *values))
    return out[1:] if len(values) > 1 else out[1]


def everyone(x, axis, size):
    return lax.all_to_all(
        jnp.broadcast_to(x[None], (size, *x.shape)), axis, split_axis=0, concat_axis=0, tiled=True
    )


def local(face_blocks, face_elems, coarse_slot, prolong, fine_residual, block_inverse):
    wide = lax.axis_size("wide")
    narrow = lax.axis_size("narrow")
    dev_rows = fine_residual.shape[0]
    faces = face_blocks.shape[0]
    coarse = prolong.shape[1]
    cap = max(2, (2 * faces + wide - 1) // wide)
    slots = round_up(cap, PAIR)
    plan = send_plan(wide, slots)

    fetch, count, *operands, p32 = place_faces(
        face_elems, coarse_slot, prolong, dev_rows * narrow, wide, slots
    )
    parts = []
    for i, piece in enumerate(plan):
        block = galerkin(face_blocks, operands, fetch, count, slots, piece)
        fetch = after(block, fetch)
        pairs = [(w, w ^ piece[0]) for w in range(wide)]
        parts.append(lax.ppermute(block, "wide", pairs))
        if i == 0:
            fine_residual, face_elems = after(block, fine_residual, face_elems)
            inverse = jnp.transpose(block_inverse, (1, 0, 2))
            rhs, sweep_one, copies = sweep_one_of(fine_residual, p32, inverse, wide)
            fetch = after(sweep_one, fetch)
            iterate = lax.all_to_all(copies, "wide", split_axis=0, concat_axis=0, tiled=True)
    parts.append(galerkin(face_blocks, operands, fetch, count, slots, (0, 0, slots)))
    pieces = [*plan, (0, 0, slots)]
    iterate, face_elems = after(parts[-1], iterate, face_elems)
    iterate = everyone(iterate.reshape(wide * dev_rows, coarse), "narrow", narrow)
    row, col = face_rows(face_elems, coarse_slot, dev_rows, narrow, wide)
    iterate = iterate.reshape(-1, coarse)
    vectors = jnp.dot(jnp.take(iterate, col, axis=0), prolong.T, precision=PRECISE)
    results = products(face_blocks, vectors, p32)
    total = iterate.shape[0]
    selector = lax.broadcasted_iota(jnp.int32, (total, faces), 0) == row[None, :]
    sums = jnp.dot(selector.astype(F32), results, precision=PRECISE)[:, :coarse]
    sums = sums.reshape(narrow, wide * dev_rows, coarse)
    sums = lax.all_to_all(sums, "narrow", split_axis=0, concat_axis=0, tiled=True)
    sums = jnp.sum(sums, axis=0).reshape(wide, dev_rows, coarse)
    sums = lax.all_to_all(sums, "wide", split_axis=0, concat_axis=0, tiled=True)
    correction = sweep_two_of(sums, rhs, sweep_one, prolong.T, inverse)
    owned = unpack(parts, pieces, cap, coarse, wide)
    return (correction, owned)


def solution(mesh):
    placed = (
        P(BOTH, None, None),
        P(BOTH, None),
        P(),
        P(),
        P(BOTH, None),
        P(BOTH, None, None),
    )
    return jax.shard_map(
        local,
        mesh=mesh,
        in_specs=placed,
        out_specs=(P(BOTH, None), P(BOTH, None, None)),
        check_vma=False,
    )
```

```python
import functools

import jax
import jax.numpy as jnp
from jax import lax
from jax.experimental import pallas as pl
from jax.experimental.pallas import tpu as pltpu
from jax.sharding import PartitionSpec as P

DAMPING = 0.7
PRECISE = lax.Precision.HIGHEST
BOTH = ("wide", "narrow")
LANES = 128
PAIR = 2
WHOLE_VMEM = 67043328
F32 = jnp.float32
BF16 = jnp.bfloat16


def round_up(value, unit):
    return (value + unit - 1) // unit * unit


def split(x):
    high = x.astype(BF16)
    return high, (x - high.astype(F32)).astype(BF16)


dot = functools.partial(jnp.dot, preferred_element_type=F32)


def send_plan(wide, cap):
    offsets = sorted(range(1, wide), key=lambda k: (-k.bit_length(), k))
    first = min(PAIR, cap)
    plan = [(offsets[0], 0, first)]
    if cap > first:
        plan.append((offsets[0], first, cap - first))
    return plan + [(k, 0, cap) for k in offsets[1:]]


def place_kernel(
    owner_rows, cap, elems_in, slots_in, me, pt_in, fetch, count, ph, pl_, th, tl, p32, elems, slots, pt, wide_pt, sems
):
    faces, wide = elems.shape[1], count.shape[0]
    sources = ((elems_in, elems), (slots_in, slots), (pt_in, pt))
    copies = [pltpu.make_async_copy(a, b, sems.at[i]) for i, (a, b) in enumerate(sources)]
    for copy in copies:
        copy.start()
    wide_pt[...] = jnp.zeros_like(wide_pt)
    for copy in copies:
        copy.wait()

    def put(f, c):
        owner = lax.div(slots[elems[0, f]], owner_rows)
        at = owner ^ me[0]
        rank = count[at]
        count[at] = rank + 1
        fetch[at * cap + rank] = f
        return c

    for k in range(wide):
        count[k] = 0
    lax.fori_loop(0, faces, put, 0, unroll=8)

    def fill(k, c):
        for r in range(cap):

            @pl.when(r >= count[k])
            def _(r=r):
                fetch[k * cap + r] = fetch[k * cap + r - PAIR] if r >= PAIR else 0

        return c

    lax.fori_loop(0, wide, fill, 0)
    rows, fine = th.shape
    wide_pt[: pt.shape[0], :fine] = pt[...]
    th[...], tl[...] = split(wide_pt[:rows, :fine])
    p32[...] = wide_pt[...].T[:fine]
    ph[...], pl_[...] = split(p32[...])


SMEM = pl.BlockSpec(memory_space=pltpu.SMEM)
VMEM = pl.BlockSpec(memory_space=pltpu.VMEM)
HBM = pl.BlockSpec(memory_space=pltpu.HBM)


def ints(n):
    return jax.ShapeDtypeStruct((n,), jnp.int32)


def place_faces(face_elems, coarse_slot, prolong, owner_rows, wide, cap):
    fine, coarse = prolong.shape
    rows = round_up(coarse, 8)
    halves = lambda *s: jax.ShapeDtypeStruct(s, BF16)
    me = lax.axis_index("wide").astype(jnp.int32).reshape(1)
    return pl.pallas_call(
        functools.partial(place_kernel, owner_rows, cap),
        out_shape=(
            ints(wide * cap),
            ints(wide),
            halves(fine, 2 * LANES),
            halves(fine, 2 * LANES),
            halves(rows, fine),
            halves(rows, fine),
            jax.ShapeDtypeStruct((fine, 2 * LANES), F32),
        ),
        in_specs=[HBM, HBM, SMEM, HBM],
        out_specs=(SMEM, SMEM, VMEM, VMEM, VMEM, VMEM, VMEM),
        scratch_shapes=[
            pltpu.SMEM(face_elems.shape[::-1], jnp.int32),
            pltpu.SMEM(coarse_slot.shape, jnp.int32),
            pltpu.VMEM((coarse, fine), F32),
            pltpu.VMEM((2 * LANES, round_up(fine, LANES)), F32),
            pltpu.SemaphoreType.DMA((3,)),
        ],
        compiler_params=pltpu.CompilerParams(vmem_limit_bytes=WHOLE_VMEM),
        name="place_faces",
    )(face_elems.T, coarse_slot, me, prolong.T)


def apply_blocks(blocks, vectors):
    coarse = blocks.shape[0]
    lane = lax.broadcasted_iota(jnp.int32, vectors.shape, 1)

    def add(n, out):
        value = jnp.sum(blocks[n] * vectors, axis=1, keepdims=True)
        return jnp.where(lane == n, value, out)

    return lax.fori_loop(0, coarse, add, jnp.zeros_like(vectors), unroll=9)


def sweep_one_kernel(residual, p32, blocks, rhs, sweep, copies):
    rhs[...] = jnp.dot(residual[...], p32[...], precision=PRECISE, preferred_element_type=F32)
    sweep[...] = DAMPING * apply_blocks(blocks, rhs[:, : blocks.shape[0]])
    copies[...] = jnp.broadcast_to(sweep[...][None], copies.shape)


def sweep_one_of(residual, p32, blocks, wide):
    rows, coarse = residual.shape[0], blocks.shape[0]
    return pl.pallas_call(
        sweep_one_kernel,
        out_shape=(
            jax.ShapeDtypeStruct((rows, p32.shape[1]), F32),
            jax.ShapeDtypeStruct((rows, coarse), F32),
            jax.ShapeDtypeStruct((wide, rows, coarse), F32),
        ),
        in_specs=[VMEM] * 3,
        out_specs=(VMEM, VMEM, VMEM),
        compiler_params=pltpu.CompilerParams(vmem_limit_bytes=WHOLE_VMEM),
        name="sweep_one",
    )(residual, p32, blocks)


def sweep_two_kernel(sums, rhs, sweep, pt, blocks, out):
    coarse = blocks.shape[0]
    update = (1.0 - DAMPING) * rhs[:, :coarse] - jnp.sum(sums[...], axis=0)[:, :coarse]
    last = sweep[...] + DAMPING * apply_blocks(blocks, update)
    out[...] = jnp.dot(last, pt[...], precision=PRECISE, preferred_element_type=F32)


def sweep_two_of(sums, rhs, sweep, pt, blocks):
    return pl.pallas_call(
        sweep_two_kernel,
        out_shape=jax.ShapeDtypeStruct((rhs.shape[0], pt.shape[1]), F32),
        in_specs=[VMEM] * 5,
        out_specs=VMEM,
        compiler_params=pltpu.CompilerParams(vmem_limit_bytes=8 << 20),
        name="sweep_two",
    )(sums, rhs, sweep, pt, blocks)


def product_kernel(dev_rows, narrow, wide, elems, slots, a_ref, x_ref, p_ref, pt_ref, sums):
    step = pl.program_id(0)
    group = a_ref.shape[0]
    owner_rows = dev_rows * narrow

    def moved(r):
        owner = lax.div(r, owner_rows)
        inner = r - owner * owner_rows
        n = lax.div(inner, dev_rows)
        return (n * wide + owner) * dev_rows + inner - n * dev_rows

    @pl.when(step == 0)
    def _():
        sums[...] = jnp.zeros_like(sums)

    faces = [step * group + j for j in range(group)]
    vectors = [x_ref[pl.ds(moved(slots[elems[1, f]]), 1), :] for f in faces]
    vectors = jnp.concatenate(vectors, axis=0)
    vectors = jnp.dot(vectors, pt_ref[...], precision=PRECISE, preferred_element_type=F32)
    for j, f in enumerate(faces):
        applied = jnp.sum(a_ref[j] * vectors[j : j + 1, :], axis=1, keepdims=True)
        row = pl.ds(moved(slots[elems[0, f]]), 1)
        sums[row, :] = sums[row, :] + jnp.sum(p_ref[...] * applied, axis=0, keepdims=True)


def products(face_blocks, face_elems, coarse_slot, iterate, p32, pt, dev_rows, narrow, wide):
    faces, fine, _ = face_blocks.shape
    group = 8 if faces % 8 == 0 else faces
    return pl.pallas_call(
        functools.partial(product_kernel, dev_rows, narrow, wide),
        out_shape=jax.ShapeDtypeStruct((iterate.shape[0], p32.shape[1]), F32),
        grid=(faces // group,),
        in_specs=[
            SMEM,
            SMEM,
            pl.BlockSpec((group, fine, fine), lambda s: (s, 0, 0)),
            VMEM,
            VMEM,
            VMEM,
        ],
        out_specs=VMEM,
        compiler_params=pltpu.CompilerParams(vmem_limit_bytes=48 << 20),
        cost_estimate=pl.CostEstimate(
            flops=4 * faces * fine * fine, bytes_accessed=4 * faces * fine * fine, transcendentals=0
        ),
        name="products",
    )(face_elems.T, coarse_slot, face_blocks, iterate, p32, pt)


def galerkin_kernel(at, first, fetch, count, *refs):
    a_refs, (ph, pl_, th, tl, o_ref) = refs[:PAIR], refs[PAIR:]
    rank = first + pl.program_id(0) * PAIR
    rows = th.shape[0]
    full = ph.shape[0] // (2 * LANES) * 2 * LANES

    @pl.when(rank >= count[at])
    def _():
        o_ref[...] = jnp.zeros_like(o_ref)

    @pl.when(rank < count[at])
    def _():
        left = []
        for j in range(PAIR):
            ah, al = split(a_refs[j][0])
            left.append(
                jnp.concatenate(
                    (ah[:, :full], al[:, :full], ah[:, :full], ah[:, full:], al[:, full:], ah[:, full:]),
                    axis=1,
                )
            )
        right = (ph[:full], ph[:full], pl_[:full], ph[full:], ph[full:], pl_[full:])
        applied = dot(jnp.concatenate(left, axis=0), jnp.concatenate(right, axis=0))
        fine = ph.shape[0]
        for j in range(PAIR):
            bh, bl = split(applied[j * fine : (j + 1) * fine])
            block = dot(th[...], bh) + (dot(tl[...], bh) + dot(th[...], bl))
            if j:
                block = jnp.where(rank + j < count[at], block, 0.0)
            o_ref[j, :rows, :] = block[:, :LANES]
            rest = block[:, LANES:]
            turned = rest[:LANES].T[:8]
            corner = pltpu.roll(rest[LANES:rows], 0, 1, stride=8, stride_axis=0)
            corner = jnp.sum(corner, axis=0, keepdims=True)
            last = lax.broadcasted_iota(jnp.int32, (8, LANES), 0) == 7
            o_ref[j, rows:, :] = jnp.where(last, corner, turned)


def galerkin(face_blocks, operands, fetch, count, cap, piece):
    at, first, ranks = piece
    fine = face_blocks.shape[1]
    ph, _, th, _ = operands
    width, rows = ph.shape[1], th.shape[0]
    face = lambda j: lambda s, fetch, count: (fetch[at * cap + first + s * PAIR + j], 0, 0)
    return pl.pallas_call(
        functools.partial(galerkin_kernel, at, first),
        out_shape=jax.ShapeDtypeStruct((ranks, rows + 8, LANES), F32),
        grid_spec=pltpu.PrefetchScalarGridSpec(
            num_scalar_prefetch=2,
            grid=(ranks // PAIR,),
            in_specs=[pl.BlockSpec((1, fine, fine), face(j)) for j in range(PAIR)]
            + [VMEM] * 4,
            out_specs=pl.BlockSpec((PAIR, rows + 8, LANES), lambda s, fetch, count: (s, 0, 0)),
        ),
        compiler_params=pltpu.CompilerParams(vmem_limit_bytes=WHOLE_VMEM),
        cost_estimate=pl.CostEstimate(
            flops=ranks * 6 * fine * fine * width,
            bytes_accessed=ranks * 4 * (fine * fine + rows * LANES),
            transcendentals=0,
        ),
        name="galerkin",
    )(fetch, count, *[face_blocks] * PAIR, *operands)


def unpack_kernel(pieces, cap, coarse, me, *refs):
    parts, out = refs[: len(pieces)], refs[len(pieces)]
    buf, turned, sems = refs[len(pieces) + 1 :]
    step = pl.program_id(0)
    total, rows, _ = buf.shape
    main = rows - 8
    size = out.shape[0]
    groups = [(at, min(size, main - at)) for at in range(0, main, size)] + [(main, 8)]
    tail = len(groups) - 1

    def copies(g):
        at, extent = groups[g]
        for part, (offset, first, ranks) in zip(parts, pieces):
            ranks = min(ranks, cap - first)
            source = part.at[pl.ds(0, ranks), pl.ds(at, extent), :]
            target = buf.at[pl.ds((me[0] ^ offset) * cap + first, ranks), pl.ds(at, extent), :]
            yield pltpu.make_async_copy(source, target, sems.at[g])

    flat = buf.reshape(total * rows, LANES)

    def turn(r):
        x = flat[pl.ds(r, total, stride=rows), :]
        if total < LANES:
            x = jnp.concatenate([x, jnp.zeros((LANES - total, LANES), F32)], axis=0)
        return x.T

    @pl.when(step == 0)
    def _():
        for g in [tail, *range(tail)]:
            for copy in copies(g):
                copy.start()
        for copy in copies(tail):
            copy.wait()
        for k in range(7):
            turned[pl.ds(k, LANES, stride=8), :] = turn(main + k)
        turned[pl.ds(8 * LANES, 64), :] = turn(main + 7)[:64]

    for g in range(tail):

        @pl.when(step == g)
        def _(g=g):
            for copy in copies(g):
                copy.wait()

    for i in range(size):
        a = jnp.minimum(step * size + i, main - 1)
        out[i, :LANES, :] = turn(a)[:, :total]
        out[i, LANES:coarse, :] = turned[pl.ds(pl.multiple_of(a * 8, 8), 8), :][
            : coarse - LANES, :total
        ]


def unpack(parts, pieces, cap, coarse, wide, size=24):
    rows = parts[0].shape[1]
    total = wide * cap
    groups = pl.cdiv(rows - 8, size)
    me = lax.axis_index("wide").astype(jnp.int32).reshape(1)
    out = pl.pallas_call(
        functools.partial(unpack_kernel, pieces, cap, coarse),
        out_shape=jax.ShapeDtypeStruct((coarse, coarse, total), F32),
        grid=(groups,),
        in_specs=[pl.BlockSpec(memory_space=pltpu.SMEM)]
        + [pl.BlockSpec(memory_space=pl.ANY)] * len(parts),
        out_specs=pl.BlockSpec((size, coarse, total), lambda s: (s, 0, 0)),
        scratch_shapes=[
            pltpu.VMEM((total, rows, LANES), F32),
            pltpu.VMEM((8 * LANES + 64, LANES), F32),
            pltpu.SemaphoreType.DMA((groups + 1,)),
        ],
        compiler_params=pltpu.CompilerParams(vmem_limit_bytes=32 << 20),
        cost_estimate=pl.CostEstimate(
            flops=0, bytes_accessed=total * 8 * rows * LANES, transcendentals=0
        ),
        name="unpack",
    )(me, *parts)
    return jnp.transpose(out, (2, 0, 1))


def after(first, *values):
    out = lax.optimization_barrier((first, *values))
    return out[1:] if len(values) > 1 else out[1]


def everyone(x, axis, size):
    return lax.all_to_all(
        jnp.broadcast_to(x[None], (size, *x.shape)), axis, split_axis=0, concat_axis=0, tiled=True
    )


def local(face_blocks, face_elems, coarse_slot, prolong, fine_residual, block_inverse):
    wide = lax.axis_size("wide")
    narrow = lax.axis_size("narrow")
    dev_rows = fine_residual.shape[0]
    faces = face_blocks.shape[0]
    coarse = prolong.shape[1]
    cap = max(2, (2 * faces + wide - 1) // wide)
    slots = round_up(cap, PAIR)
    plan = send_plan(wide, slots)

    fetch, count, *operands, p32 = place_faces(
        face_elems, coarse_slot, prolong, dev_rows * narrow, wide, slots
    )
    parts = []
    for i, piece in enumerate(plan):
        block = galerkin(face_blocks, operands, fetch, count, slots, piece)
        fetch = after(block, fetch)
        pairs = [(w, w ^ piece[0]) for w in range(wide)]
        parts.append(lax.ppermute(block, "wide", pairs))
        if i == 1:
            fine_residual, face_elems = after(block, fine_residual, face_elems)
            inverse = jnp.transpose(block_inverse, (1, 0, 2))
            rhs, sweep_one, copies = sweep_one_of(fine_residual, p32, inverse, wide)
            fetch = after(sweep_one, fetch)
            iterate = lax.all_to_all(copies, "wide", split_axis=0, concat_axis=0, tiled=True)
    iterate = after(block, iterate)
    iterate = everyone(iterate.reshape(wide * dev_rows, coarse), "narrow", narrow)
    parts.append(galerkin(face_blocks, operands, fetch, count, slots, (0, 0, slots)))
    pieces = [*plan, (0, 0, slots)]
    iterate = after(parts[-1], iterate).reshape(-1, coarse)
    sums = products(
        face_blocks, face_elems, coarse_slot, iterate, p32, prolong.T, dev_rows, narrow, wide
    ).reshape(narrow, wide * dev_rows, -1)
    sums = lax.all_to_all(sums, "narrow", split_axis=0, concat_axis=0, tiled=True)
    sums = jnp.sum(sums, axis=0).reshape(wide, dev_rows, -1)
    sums = lax.all_to_all(sums, "wide", split_axis=0, concat_axis=0, tiled=True)
    owned = unpack(parts, pieces, cap, coarse, wide)
    correction = sweep_two_of(after(owned, sums), rhs, sweep_one, prolong.T, inverse)
    return (correction, owned)


def solution(mesh):
    placed = (
        P(BOTH, None, None),
        P(BOTH, None),
        P(),
        P(),
        P(BOTH, None),
        P(BOTH, None, None),
    )
    return jax.shard_map(
        local,
        mesh=mesh,
        in_specs=placed,
        out_specs=(P(BOTH, None), P(BOTH, None, None)),
        check_vma=False,
    )
```

```python
import functools

import jax
import jax.numpy as jnp
from jax import lax
from jax.experimental import pallas as pl
from jax.experimental.pallas import tpu as pltpu
from jax.sharding import PartitionSpec as P

DAMPING = 0.7
PRECISE = lax.Precision.HIGHEST
BOTH = ("wide", "narrow")
LANES = 128
PAIR = 2
WHOLE_VMEM = 67043328
F32 = jnp.float32
BF16 = jnp.bfloat16


def round_up(value, unit):
    return (value + unit - 1) // unit * unit


def split(x):
    high = x.astype(BF16)
    return high, (x - high.astype(F32)).astype(BF16)


dot = functools.partial(jnp.dot, preferred_element_type=F32)


def send_plan(wide, cap):
    offsets = sorted(range(1, wide), key=lambda k: (-k.bit_length(), k))
    first = min(PAIR, cap)
    plan = [(offsets[0], 0, first)]
    if cap > first:
        plan.append((offsets[0], first, cap - first))
    return plan + [(k, 0, cap) for k in offsets[1:]]


def place_kernel(
    owner_rows, cap, elems_in, slots_in, me, pt_in, fetch, count, ph, pl_, th, tl, p32, elems, slots, pt, wide_pt, sems
):
    faces, wide = elems.shape[1], count.shape[0]
    sources = ((elems_in, elems), (slots_in, slots), (pt_in, pt))
    copies = [pltpu.make_async_copy(a, b, sems.at[i]) for i, (a, b) in enumerate(sources)]
    for copy in copies:
        copy.start()
    wide_pt[...] = jnp.zeros_like(wide_pt)
    for copy in copies:
        copy.wait()

    def put(f, c):
        owner = lax.div(slots[elems[0, f]], owner_rows)
        at = owner ^ me[0]
        rank = count[at]
        count[at] = rank + 1
        fetch[at * cap + rank] = f
        return c

    for k in range(wide):
        count[k] = 0
    lax.fori_loop(0, faces, put, 0, unroll=8)

    def fill(k, c):
        for r in range(cap):

            @pl.when(r >= count[k])
            def _(r=r):
                fetch[k * cap + r] = fetch[k * cap + r - PAIR] if r >= PAIR else 0

        return c

    lax.fori_loop(0, wide, fill, 0)
    rows, fine = th.shape
    wide_pt[: pt.shape[0], :fine] = pt[...]
    th[...], tl[...] = split(wide_pt[:rows, :fine])
    p32[...] = wide_pt[...].T[:fine]
    ph[...], pl_[...] = split(p32[...])


SMEM = pl.BlockSpec(memory_space=pltpu.SMEM)
VMEM = pl.BlockSpec(memory_space=pltpu.VMEM)
HBM = pl.BlockSpec(memory_space=pltpu.HBM)


def ints(n):
    return jax.ShapeDtypeStruct((n,), jnp.int32)


def place_faces(face_elems, coarse_slot, prolong, owner_rows, wide, cap):
    fine, coarse = prolong.shape
    rows = round_up(coarse, 8)
    halves = lambda *s: jax.ShapeDtypeStruct(s, BF16)
    me = lax.axis_index("wide").astype(jnp.int32).reshape(1)
    return pl.pallas_call(
        functools.partial(place_kernel, owner_rows, cap),
        out_shape=(
            ints(wide * cap),
            ints(wide),
            halves(fine, 2 * LANES),
            halves(fine, 2 * LANES),
            halves(rows, fine),
            halves(rows, fine),
            jax.ShapeDtypeStruct((fine, 2 * LANES), F32),
        ),
        in_specs=[HBM, HBM, SMEM, HBM],
        out_specs=(SMEM, SMEM, VMEM, VMEM, VMEM, VMEM, VMEM),
        scratch_shapes=[
            pltpu.SMEM(face_elems.shape[::-1], jnp.int32),
            pltpu.SMEM(coarse_slot.shape, jnp.int32),
            pltpu.VMEM((coarse, fine), F32),
            pltpu.VMEM((2 * LANES, round_up(fine, LANES)), F32),
            pltpu.SemaphoreType.DMA((3,)),
        ],
        compiler_params=pltpu.CompilerParams(vmem_limit_bytes=WHOLE_VMEM),
        name="place_faces",
    )(face_elems.T, coarse_slot, me, prolong.T)


def apply_blocks(blocks, vectors):
    coarse = blocks.shape[0]
    lane = lax.broadcasted_iota(jnp.int32, vectors.shape, 1)

    def add(n, out):
        value = jnp.sum(blocks[n] * vectors, axis=1, keepdims=True)
        return jnp.where(lane == n, value, out)

    return lax.fori_loop(0, coarse, add, jnp.zeros_like(vectors), unroll=9)


def sweep_one_kernel(residual, p32, blocks, rhs, sweep, copies):
    rhs[...] = jnp.dot(residual[...], p32[...], precision=PRECISE, preferred_element_type=F32)
    sweep[...] = DAMPING * apply_blocks(blocks, rhs[:, : blocks.shape[0]])
    copies[...] = jnp.broadcast_to(sweep[...][None], copies.shape)


def sweep_one_of(residual, p32, blocks, wide):
    rows, coarse = residual.shape[0], blocks.shape[0]
    return pl.pallas_call(
        sweep_one_kernel,
        out_shape=(
            jax.ShapeDtypeStruct((rows, p32.shape[1]), F32),
            jax.ShapeDtypeStruct((rows, coarse), F32),
            jax.ShapeDtypeStruct((wide, rows, coarse), F32),
        ),
        in_specs=[VMEM] * 3,
        out_specs=(VMEM, VMEM, VMEM),
        compiler_params=pltpu.CompilerParams(vmem_limit_bytes=WHOLE_VMEM),
        name="sweep_one",
    )(residual, p32, blocks)


def sweep_two_kernel(sums, rhs, sweep, pt, blocks, out):
    coarse = blocks.shape[0]
    update = (1.0 - DAMPING) * rhs[:, :coarse] - jnp.sum(sums[...], axis=0)[:, :coarse]
    last = sweep[...] + DAMPING * apply_blocks(blocks, update)
    out[...] = jnp.dot(last, pt[...], precision=PRECISE, preferred_element_type=F32)


def product_kernel(dev_rows, narrow, wide, elems, slots, a_ref, x_ref, p_ref, pt_ref, sums):
    step = pl.program_id(0)
    group = a_ref.shape[0]
    owner_rows = dev_rows * narrow

    def moved(r):
        owner = lax.div(r, owner_rows)
        inner = r - owner * owner_rows
        n = lax.div(inner, dev_rows)
        return (n * wide + owner) * dev_rows + inner - n * dev_rows

    @pl.when(step == 0)
    def _():
        sums[...] = jnp.zeros_like(sums)

    faces = [step * group + j for j in range(group)]
    vectors = [x_ref[pl.ds(moved(slots[elems[1, f]]), 1), :] for f in faces]
    vectors = jnp.concatenate(vectors, axis=0)
    vectors = jnp.dot(vectors, pt_ref[...], precision=PRECISE, preferred_element_type=F32)
    for j, f in enumerate(faces):
        applied = jnp.sum(a_ref[j] * vectors[j : j + 1, :], axis=1, keepdims=True)
        row = pl.ds(moved(slots[elems[0, f]]), 1)
        sums[row, :] = sums[row, :] + jnp.sum(p_ref[...] * applied, axis=0, keepdims=True)


def products(face_blocks, face_elems, coarse_slot, iterate, p32, pt, dev_rows, narrow, wide):
    faces, fine, _ = face_blocks.shape
    group = 8 if faces % 8 == 0 else faces
    return pl.pallas_call(
        functools.partial(product_kernel, dev_rows, narrow, wide),
        out_shape=jax.ShapeDtypeStruct((iterate.shape[0], p32.shape[1]), F32),
        grid=(faces // group,),
        in_specs=[
            SMEM,
            SMEM,
            pl.BlockSpec((group, fine, fine), lambda s: (s, 0, 0)),
            VMEM,
            VMEM,
            VMEM,
        ],
        out_specs=VMEM,
        compiler_params=pltpu.CompilerParams(vmem_limit_bytes=48 << 20),
        cost_estimate=pl.CostEstimate(
            flops=4 * faces * fine * fine, bytes_accessed=4 * faces * fine * fine, transcendentals=0
        ),
        name="products",
    )(face_elems.T, coarse_slot, face_blocks, iterate, p32, pt)


def galerkin_kernel(at, first, fetch, count, *refs):
    a_refs, (ph, pl_, th, tl, o_ref) = refs[:PAIR], refs[PAIR:]
    rank = first + pl.program_id(0) * PAIR
    rows = th.shape[0]
    full = ph.shape[0] // (2 * LANES) * 2 * LANES

    @pl.when(rank >= count[at])
    def _():
        o_ref[...] = jnp.zeros_like(o_ref)

    @pl.when(rank < count[at])
    def _():
        left = []
        for j in range(PAIR):
            ah, al = split(a_refs[j][0])
            left.append(
                jnp.concatenate(
                    (ah[:, :full], al[:, :full], ah[:, :full], ah[:, full:], al[:, full:], ah[:, full:]),
                    axis=1,
                )
            )
        right = (ph[:full], ph[:full], pl_[:full], ph[full:], ph[full:], pl_[full:])
        applied = dot(jnp.concatenate(left, axis=0), jnp.concatenate(right, axis=0))
        fine = ph.shape[0]
        for j in range(PAIR):
            bh, bl = split(applied[j * fine : (j + 1) * fine])
            block = dot(th[...], bh) + (dot(tl[...], bh) + dot(th[...], bl))
            if j:
                block = jnp.where(rank + j < count[at], block, 0.0)
            o_ref[j, :rows, :] = block[:, :LANES]
            rest = block[:, LANES:]
            turned = rest[:LANES].T[:8]
            corner = pltpu.roll(rest[LANES:rows], 0, 1, stride=8, stride_axis=0)
            corner = jnp.sum(corner, axis=0, keepdims=True)
            last = lax.broadcasted_iota(jnp.int32, (8, LANES), 0) == 7
            o_ref[j, rows:, :] = jnp.where(last, corner, turned)


def galerkin(face_blocks, operands, fetch, count, cap, piece):
    at, first, ranks = piece
    fine = face_blocks.shape[1]
    ph, _, th, _ = operands
    width, rows = ph.shape[1], th.shape[0]
    face = lambda j: lambda s, fetch, count: (fetch[at * cap + first + s * PAIR + j], 0, 0)
    return pl.pallas_call(
        functools.partial(galerkin_kernel, at, first),
        out_shape=jax.ShapeDtypeStruct((ranks, rows + 8, LANES), F32),
        grid_spec=pltpu.PrefetchScalarGridSpec(
            num_scalar_prefetch=2,
            grid=(ranks // PAIR,),
            in_specs=[pl.BlockSpec((1, fine, fine), face(j)) for j in range(PAIR)]
            + [VMEM] * 4,
            out_specs=pl.BlockSpec((PAIR, rows + 8, LANES), lambda s, fetch, count: (s, 0, 0)),
        ),
        compiler_params=pltpu.CompilerParams(vmem_limit_bytes=WHOLE_VMEM),
        cost_estimate=pl.CostEstimate(
            flops=ranks * 6 * fine * fine * width,
            bytes_accessed=ranks * 4 * (fine * fine + rows * LANES),
            transcendentals=0,
        ),
        name="galerkin",
    )(fetch, count, *[face_blocks] * PAIR, *operands)


def unpack_kernel(pieces, cap, coarse, me, sums, rhs, sweep, pt, blocks, *refs):
    parts, (out, correction) = refs[: len(pieces)], refs[len(pieces) : len(pieces) + 2]
    buf, turned, sems = refs[len(pieces) + 2 :]
    step = pl.program_id(0)
    total, rows, _ = buf.shape
    main = rows - 8
    size = out.shape[0]
    groups = [(at, min(size, main - at)) for at in range(0, main, size)] + [(main, 8)]
    tail = len(groups) - 1

    def copies(g):
        at, extent = groups[g]
        for part, (offset, first, ranks) in zip(parts, pieces):
            ranks = min(ranks, cap - first)
            source = part.at[pl.ds(0, ranks), pl.ds(at, extent), :]
            target = buf.at[pl.ds((me[0] ^ offset) * cap + first, ranks), pl.ds(at, extent), :]
            yield pltpu.make_async_copy(source, target, sems.at[g])

    flat = buf.reshape(total * rows, LANES)

    def turn(r):
        x = flat[pl.ds(r, total, stride=rows), :]
        if total < LANES:
            x = jnp.concatenate([x, jnp.zeros((LANES - total, LANES), F32)], axis=0)
        return x.T

    @pl.when(step == 0)
    def _():
        for g in [tail, *range(tail)]:
            for copy in copies(g):
                copy.start()
        sweep_two_kernel(sums, rhs, sweep, pt, blocks, correction)
        for copy in copies(tail):
            copy.wait()
        for k in range(7):
            turned[pl.ds(k, LANES, stride=8), :] = turn(main + k)
        turned[pl.ds(8 * LANES, 64), :] = turn(main + 7)[:64]

    for g in range(tail):

        @pl.when(step == g)
        def _(g=g):
            for copy in copies(g):
                copy.wait()

    for i in range(size):
        a = jnp.minimum(step * size + i, main - 1)
        out[i, :LANES, :] = turn(a)[:, :total]
        out[i, LANES:coarse, :] = turned[pl.ds(pl.multiple_of(a * 8, 8), 8), :][
            : coarse - LANES, :total
        ]


def unpack(parts, pieces, cap, coarse, wide, sweep_operands, size=24):
    rows = parts[0].shape[1]
    total = wide * cap
    groups = pl.cdiv(rows - 8, size)
    me = lax.axis_index("wide").astype(jnp.int32).reshape(1)
    _, rhs, _, pt, _ = sweep_operands
    out, correction = pl.pallas_call(
        functools.partial(unpack_kernel, pieces, cap, coarse),
        out_shape=(
            jax.ShapeDtypeStruct((coarse, coarse, total), F32),
            jax.ShapeDtypeStruct((rhs.shape[0], pt.shape[1]), F32),
        ),
        grid=(groups,),
        in_specs=[SMEM] + [VMEM] * 5 + [pl.BlockSpec(memory_space=pl.ANY)] * len(parts),
        out_specs=(pl.BlockSpec((size, coarse, total), lambda s: (s, 0, 0)), VMEM),
        scratch_shapes=[
            pltpu.VMEM((total, rows, LANES), F32),
            pltpu.VMEM((8 * LANES + 64, LANES), F32),
            pltpu.SemaphoreType.DMA((groups + 1,)),
        ],
        compiler_params=pltpu.CompilerParams(vmem_limit_bytes=32 << 20),
        cost_estimate=pl.CostEstimate(
            flops=0, bytes_accessed=total * 8 * rows * LANES, transcendentals=0
        ),
        name="unpack",
    )(me, *sweep_operands, *parts)
    return correction, jnp.transpose(out, (2, 0, 1))


def after(first, *values):
    out = lax.optimization_barrier((first, *values))
    return out[1:] if len(values) > 1 else out[1]


def everyone(x, axis, size):
    return lax.all_to_all(
        jnp.broadcast_to(x[None], (size, *x.shape)), axis, split_axis=0, concat_axis=0, tiled=True
    )


def local(face_blocks, face_elems, coarse_slot, prolong, fine_residual, block_inverse):
    wide = lax.axis_size("wide")
    narrow = lax.axis_size("narrow")
    dev_rows = fine_residual.shape[0]
    faces = face_blocks.shape[0]
    coarse = prolong.shape[1]
    cap = max(2, (2 * faces + wide - 1) // wide)
    slots = round_up(cap, PAIR)
    plan = send_plan(wide, slots)

    fetch, count, *operands, p32 = place_faces(
        face_elems, coarse_slot, prolong, dev_rows * narrow, wide, slots
    )
    parts = []
    for i, piece in enumerate(plan):
        block = galerkin(face_blocks, operands, fetch, count, slots, piece)
        fetch = after(block, fetch)
        pairs = [(w, w ^ piece[0]) for w in range(wide)]
        parts.append(lax.ppermute(block, "wide", pairs))
        if i == 1:
            fine_residual, face_elems = after(block, fine_residual, face_elems)
            inverse = jnp.transpose(block_inverse, (1, 0, 2))
            rhs, sweep_one, copies = sweep_one_of(fine_residual, p32, inverse, wide)
            fetch = after(sweep_one, fetch)
            iterate = lax.all_to_all(copies, "wide", split_axis=0, concat_axis=0, tiled=True)
    iterate = after(block, iterate)
    iterate = everyone(iterate.reshape(wide * dev_rows, coarse), "narrow", narrow)
    parts.append(galerkin(face_blocks, operands, fetch, count, slots, (0, 0, slots)))
    pieces = [*plan, (0, 0, slots)]
    iterate = after(parts[-1], iterate).reshape(-1, coarse)
    sums = products(
        face_blocks, face_elems, coarse_slot, iterate, p32, prolong.T, dev_rows, narrow, wide
    ).reshape(narrow, wide * dev_rows, -1)
    sums = lax.all_to_all(sums, "narrow", split_axis=0, concat_axis=0, tiled=True)
    sums = jnp.sum(sums, axis=0).reshape(wide, dev_rows, -1)
    sums = lax.all_to_all(sums, "wide", split_axis=0, concat_axis=0, tiled=True)
    correction, owned = unpack(
        parts, pieces, cap, coarse, wide, (sums, rhs, sweep_one, prolong.T, inverse)
    )
    return (correction, owned)


def solution(mesh):
    placed = (
        P(BOTH, None, None),
        P(BOTH, None),
        P(),
        P(),
        P(BOTH, None),
        P(BOTH, None, None),
    )
    return jax.shard_map(
        local,
        mesh=mesh,
        in_specs=placed,
        out_specs=(P(BOTH, None), P(BOTH, None, None)),
        check_vma=False,
    )
```
